256 devices in a mesh: gz: 4 (over x), dev: 64 (over z, y, core).
Axes of the slice: x: 4, y: 4, z: 8, core: 2. Of those that a mesh axis runs over, the one named last changes fastest.
Arguments:
- source: float32 [512, 8, 16384], P(None, None, ('gz', 'dev')), may hold values from -6 to 6
- interior_inverse: float32 [512, 512], replicated, as said below
- coupling: float32 [512, 384], replicated, may hold values from -0.25 to 0.25
- trace_operator: float32 [384, 384], replicated, as said below
- face_ids: int32 [16384, 4], P(('gz', 'dev')), may hold values from 0 to 8191, as said below
- orientation: int32 [16384, 6], P(('gz', 'dev')), may hold values from 0 to 7
- element_scale: int32 [16384], P(('gz', 'dev')), may hold values from 1 to 4
Outputs:
- interior: float32 [512, 8, 16384], P(None, None, ('gz', 'dev'))
- side_traces: float32 [64, 8, 32768], P(None, None, ('gz', 'dev'))
- top_traces: float32 [64, 8, 16384], P(None, None, ('gz', 'dev'))
The draws below stay inside these ranges and needn't reach their ends.
Inputs may be any that keep to these rules, and one draw needn't show every extreme that they name: `face_ids`: elements come in blocks of 64 (block b of a layer is the layer's elements b * 64 onward) and a layer's side faces in blocks of 128; face f of a layer belongs to block f // 128. Columns 0 and 1 of a block's elements name each face of that block exactly once. Columns 2 and 3 of a layer's elements name each face of the layer exactly once. The elements of one block name, in columns 2 and 3, at most 1 faces of any one other block, and in every layer some block reaches 1 with some other block. `interior_inverse`: symmetric positive definite. `trace_operator`: symmetric positive definite.
All inputs are finite; a program needn't handle non-finite values.
Results may differ from the reference program's by a relative error of at most 0.0001.
Values sent between devices are 32-bit elements; how exact they have to be, the bound alone decides.
A program may use at most 64 MiB of HBM per device.

```python
import math
import jax
import jax.numpy as jnp
from jax import lax

NODES = 512
FACE_NODES = 64
RIGHT_SIDES = 8
ITERATIONS = 2
ELEMENTS_DEV = 64
FACES_DEV = 128
CAPACITY = 1
ELEMENTS = 16384
SIDE_FACES = 32768
N_GZ = 4
N_DEV = 64


def definite(key, order):
    factor = jax.random.normal(key, (order, order), jnp.float32)
    shift = 0.5
    gram = jnp.dot(factor, factor.T, precision=lax.Precision.HIGHEST) / order
    return 0.5 * (gram + gram.T) + shift * jnp.eye(order, dtype=jnp.float32)


def draw_interior_inverse(key, part):
    return definite(jax.random.fold_in(key, 11), NODES)


def draw_trace_operator(key, part):
    return definite(jax.random.fold_in(key, 12), 6 * FACE_NODES)


def shuffled(key, blocks, length):
    return jax.vmap(lambda single: jax.random.permutation(single, length))(jax.random.split(key, blocks)).astype(jnp.int32)


def layer_faces(key):
    blocks = N_DEV
    length = 2 * ELEMENTS_DEV
    limit = CAPACITY
    keys = jax.random.split(key, 6)
    raw = jax.random.randint(keys[0], (blocks, blocks), max(1, limit // 2), limit + 1).astype(jnp.int32)
    upper = jnp.triu(raw, 1)
    counts = upper + upper.T
    first = jax.random.randint(keys[1], (), 0, blocks)
    other = (first + jax.random.randint(keys[2], (), 1, blocks)) % blocks
    counts = counts.at[first, other].set(limit).at[other, first].set(limit)
    identity = jnp.eye(blocks, dtype=jnp.int32)
    counts = counts * (1 - identity)
    counts = counts + identity * (length - jnp.sum(counts, axis=1))[:, None]
    ends = jnp.cumsum(counts, axis=1)
    starts = ends - counts
    placed = shuffled(keys[3], blocks, length)
    target = jnp.sum((placed[:, :, None] >= ends[:, None, :]).astype(jnp.int32), axis=2)
    within = placed - jnp.take_along_axis(starts, target, axis=1)
    column_start = jnp.cumsum(counts, axis=0) - counts
    arrival = jnp.take_along_axis(column_start, target, axis=1) + within
    settle = shuffled(keys[4], blocks, length)
    second = target * length + settle[target, arrival]
    owned = shuffled(keys[5], blocks, length)
    first_ids = jnp.arange(blocks, dtype=jnp.int32)[:, None] * length + owned
    joined = jnp.concatenate([first_ids.reshape(blocks, ELEMENTS_DEV, 2), second.reshape(blocks, ELEMENTS_DEV, 2)], axis=2)
    return joined.reshape(blocks * ELEMENTS_DEV, 4).astype(jnp.int32)


def draw_face_ids(key, part):
    layers = jax.random.split(jax.random.fold_in(key, 13), N_GZ)
    return jax.vmap(layer_faces)(layers).reshape(ELEMENTS, 4).astype(jnp.int32)


def touch_ends(entries, key, low, high):
    extent = entries.shape
    spot = [jax.random.randint(jax.random.fold_in(key, axis), (), 0, extent[axis]) for axis in range(len(extent))]
    entries = entries.at[tuple(spot)].set(low)
    longest = extent.index(max(extent))
    spot[longest] = (spot[longest] + 1) % extent[longest]
    return entries.at[tuple(spot)].set(high)


def block_scale(key, extent, cuts, low, top_value):
    loudness = 1.0
    for axis_at, parts in cuts:
        draws = jax.random.uniform(jax.random.fold_in(jax.random.fold_in(key, 6), axis_at), (parts,), jnp.float32, low / len(cuts), top_value / len(cuts))
        loudness = loudness * jnp.repeat(jnp.exp(draws), extent[axis_at] // parts).reshape((-1,) + (1,) * (len(extent) - 1 - axis_at))
    return loudness


def noise(own_key, extent, spread, most, cuts=(), kind=jnp.bfloat16):
    result = jax.random.normal(own_key, extent, jnp.float32) * spread
    if len(cuts) > 0:
        result = block_scale(own_key, extent, cuts, -0.22, 0.18) * result
    return jnp.clip(result, min=-most, max=most).astype(kind)


def setup_inputs(seed: int = 0) -> dict:
    splits = jax.random.split(jax.random.key(seed), 8)
    source = noise(splits[0], (NODES, RIGHT_SIDES, ELEMENTS), 1.0, 6.0, ((2, 256),), jnp.float32)
    interior_inverse = draw_interior_inverse(jax.random.fold_in(splits[7], 71), 0)
    coupling = noise(splits[2], (NODES, 6 * FACE_NODES), NODES ** -0.5, 0.25, (), jnp.float32)
    trace_operator = draw_trace_operator(jax.random.fold_in(splits[7], 71), 0)
    face_ids = draw_face_ids(jax.random.fold_in(splits[7], 71), 0)
    orientation = touch_ends(jax.random.randint(splits[5], (ELEMENTS, 6), 0, 8), jax.random.fold_in(splits[5], 1), 0, 7).astype(jnp.int32)
    element_scale = touch_ends(jax.random.randint(splits[6], (ELEMENTS,), 1, 5), jax.random.fold_in(splits[6], 1), 1, 4).astype(jnp.int32)
    return dict(source=source, interior_inverse=interior_inverse, coupling=coupling, trace_operator=trace_operator, face_ids=face_ids, orientation=orientation, element_scale=element_scale)


def orient_traces(traces, codes, inverse):
    side_count, face_nodes, right_count, element_count = traces.shape
    edge = math.isqrt(face_nodes)
    grid = traces.reshape(side_count, edge, edge, right_count, element_count)
    swapped = (codes // 4 % 2 == 1)[:, None, None, None, :]
    flip_first = (codes // 2 % 2 == 1)[:, None, None, None, :]
    flip_second = (codes % 2 == 1)[:, None, None, None, :]
    if inverse:
        grid = jnp.where(flip_second, grid[:, :, ::-1], grid)
        grid = jnp.where(flip_first, grid[:, ::-1], grid)
        grid = jnp.where(swapped, jnp.swapaxes(grid, 1, 2), grid)
    else:
        grid = jnp.where(swapped, jnp.swapaxes(grid, 1, 2), grid)
        grid = jnp.where(flip_first, grid[:, ::-1], grid)
        grid = jnp.where(flip_second, grid[:, :, ::-1], grid)
    return grid.reshape(side_count, face_nodes, right_count, element_count)

def element_operator(local, trace_operator, element_scale):
    side_count, face_nodes, right_count, element_count = local.shape
    flat = local.reshape(side_count * face_nodes, right_count * element_count)
    image = jnp.dot(trace_operator, flat, precision=lax.Precision.HIGHEST, preferred_element_type=jnp.float32)
    return image.reshape(local.shape) * element_scale.astype(jnp.float32)

def layer_of():
    return jnp.arange(ELEMENTS, dtype=jnp.int32) // (ELEMENTS_DEV * N_DEV)

def global_faces(face_ids):
    return face_ids + (layer_of() * (FACES_DEV * N_DEV))[:, None]

def to_faces(local, global_ids, codes):
    layer_size = ELEMENTS_DEV * N_DEV
    placed = orient_traces(local, codes, True)
    sides = jnp.zeros((FACE_NODES, RIGHT_SIDES, SIDE_FACES), jnp.float32)
    for column in range(4):
        sides = sides.at[:, :, global_ids[:, column]].add(placed[column])
    above = jnp.concatenate([placed[4][:, :, layer_size:], jnp.zeros((FACE_NODES, RIGHT_SIDES, layer_size), jnp.float32)], axis=2)
    keep = (layer_of() < N_GZ - 1).astype(jnp.float32)
    tops = (placed[5] + above) * keep
    return (sides, tops)

def to_elements(traces, global_ids, codes):
    layer_size = ELEMENTS_DEV * N_DEV
    sides, tops = traces
    below = jnp.concatenate([jnp.zeros((FACE_NODES, RIGHT_SIDES, layer_size), jnp.float32), tops[:, :, :-layer_size]], axis=2)
    pieces = [jnp.take(sides, global_ids[:, column], axis=2) for column in range(4)]
    pieces = pieces + [below, tops]
    return orient_traces(jnp.stack(pieces), codes, False)

def inner(first, second):
    return lax.optimization_barrier(jnp.sum(first[0] * second[0], axis=(0, 2))) + lax.optimization_barrier(jnp.sum(first[1] * second[1], axis=(0, 2)))

def advance(first, factor, second):
    return tuple((left + factor[None, :, None] * right for left, right in zip(first, second)))

def reference(source, interior_inverse, coupling, trace_operator, face_ids, orientation, element_scale):
    codes = orientation.T
    global_ids = global_faces(face_ids)
    solved = jnp.dot(interior_inverse, source.reshape(NODES, RIGHT_SIDES * ELEMENTS), precision=lax.Precision.HIGHEST, preferred_element_type=jnp.float32)
    condensed = lax.dot_general(coupling, solved, (((0,), (0,)), ((), ())), precision=lax.Precision.HIGHEST, preferred_element_type=jnp.float32)
    condensed = condensed.reshape(6, FACE_NODES, RIGHT_SIDES, ELEMENTS)
    residual = to_faces(condensed, global_ids, codes)
    solution = (jnp.zeros_like(residual[0]), jnp.zeros_like(residual[1]))
    direction = residual
    norm_now = inner(residual, residual)
    for step in range(ITERATIONS):
        local = to_elements(direction, global_ids, codes)
        image = to_faces(element_operator(local, trace_operator, element_scale), global_ids, codes)
        alpha = norm_now / inner(direction, image)
        solution = advance(solution, alpha, direction)
        residual = tuple((left - alpha[None, :, None] * right for left, right in zip(residual, image)))
        norm_next = inner(residual, residual)
        direction = advance(residual, norm_next / norm_now, direction)
        norm_now = norm_next
    traces = to_elements(solution, global_ids, codes)
    coupled = jnp.dot(coupling, traces.reshape(6 * FACE_NODES, RIGHT_SIDES * ELEMENTS), precision=lax.Precision.HIGHEST, preferred_element_type=jnp.float32)
    correction = jnp.dot(interior_inverse, coupled, precision=lax.Precision.HIGHEST, preferred_element_type=jnp.float32)
    interior = solved.reshape(source.shape) / element_scale.astype(jnp.float32) - correction.reshape(source.shape)
    return (interior, solution[0], solution[1])
```

```python
import functools

import jax
import jax.numpy as jnp
from jax import lax
from jax.experimental import pallas as pl
from jax.experimental.pallas import tpu as pltpu
from jax.sharding import PartitionSpec as P

MESH = pl.DeviceIdType.MESH
F32 = jnp.float32
BF16 = jnp.bfloat16
LANES = 128
ELEMENTS = 64
RIGHT = 8
NODES = 512
LOCAL = 384
ROWS = RIGHT * ELEMENTS
PAIRS = RIGHT // 2


def partner(me, turn, count):
    if count != 64:
        return (me + 1 + turn) % count
    far_z, far_y, far_core = turn // 8, turn % 8 // 2, turn % 2
    step_z = (4 + (far_z + 1) // 2 * (1 - 2 * (far_z % 2))) % 8
    step_y = (2 + (far_y + 1) // 2 * (1 - 2 * (far_y % 2))) % 4
    z = (me // 8 + step_z) % 8
    y = (me % 8 // 2 + step_y) % 4
    core = (me % 2 + 1 - far_core) % 2
    return z * 8 + y * 2 + core


def halves(value):
    high = value.astype(BF16)
    return high, (value - high.astype(F32)).astype(BF16)


def dot(left, right):
    return jnp.dot(left, right, preferred_element_type=F32)


def dot_three(left_high, left_low, right_high, right_low):
    return dot(left_high, right_high) + (dot(left_high, right_low) + dot(left_low, right_high))


def pick(onehot, value):
    high, low = halves(value)
    return dot(onehot, high) + dot(onehot, low)


def lane_of(shape):
    return lax.broadcasted_iota(jnp.int32, shape, 1)


def row_of(shape):
    return lax.broadcasted_iota(jnp.int32, shape, 0)


def swap_pair(first, second):
    low = lane_of(first.shape) < 64
    return (
        jnp.where(low, first, pltpu.roll(second, 64, 1)),
        jnp.where(low, pltpu.roll(first, 64, 1), second),
    )


def turned(value, index):
    return jnp.take_along_axis(value, index, axis=1, mode="promise_in_bounds")


def kernel(
    layers,
    blocks,
    source_hbm,
    inverse_hbm,
    coupling_hbm,
    operator_hbm,
    faces_ref,
    codes_ref,
    scale_ref,
    interior_hbm,
    sides_hbm,
    tops_hbm,
    source,
    inverse,
    coupling,
    operator,
    source_h,
    source_l,
    inverse_h,
    inverse_l,
    coupling_h,
    coupling_l,
    operator_h,
    operator_l,
    merged_h,
    merged_l,
    merged_th,
    merged_tl,
    table,
    index_to,
    index_from,
    scales,
    first,
    image,
    update,
    vector_h,
    vector_l,
    slots_first,
    slots_second,
    bottoms,
    tops,
    solved,
    moved_zero,
    moved_one,
    sides_zero,
    sides_one,
    tops_zero,
    tops_one,
    named_out,
    named_in,
    sent,
    received,
    got_bottoms,
    got_tops,
    sum_out,
    sum_in,
    layer_out,
    layer_in,
    load_sem,
    store_sem,
    named_sem,
    swap_sem,
    up_sem,
    down_sem,
    sum_sem,
    layer_sem,
):
    layer = lax.axis_index("gz")
    me = lax.axis_index("dev")
    others = blocks - 1

    barrier = pltpu.get_barrier_semaphore()

    def greet(turn, carry):
        pl.semaphore_signal(
            barrier, inc=1, device_id={"dev": partner(me, turn, blocks)}, device_id_type=MESH
        )
        return carry

    lax.fori_loop(0, others, greet, 0)
    for step in range(1, layers):
        pl.semaphore_signal(
            barrier, inc=1, device_id={"gz": (layer + step) % layers}, device_id_type=MESH
        )

    loads = [
        pltpu.make_async_copy(inverse_hbm, inverse, load_sem.at[0]),
        pltpu.make_async_copy(coupling_hbm, coupling, load_sem.at[1]),
        pltpu.make_async_copy(source_hbm, source, load_sem.at[2]),
        pltpu.make_async_copy(operator_hbm, operator, load_sem.at[3]),
    ]
    for load in loads:
        load.start()

    here = pl.ds(pl.multiple_of(me * 8, 8), 8)
    for phase in range(2):
        received[phase, here, :] = jnp.zeros((8, LANES), F32)
    named_in[me] = jnp.zeros((1, LANES), F32)

    @pl.when(layer == 0)
    def _():
        got_bottoms[...] = jnp.zeros(got_bottoms.shape, F32)

    @pl.when(layer == layers - 1)
    def _():
        got_tops[...] = jnp.zeros(got_tops.shape, F32)

    table[...] = jnp.zeros(table.shape, F32)
    faces = faces_ref[...].astype(F32)
    codes = codes_ref[...].astype(F32)
    for row in range(2):
        table[row : row + 1, 0:64] = faces[2 * row : 2 * row + 1]
        table[row : row + 1, 64:128] = faces[2 * row + 1 : 2 * row + 2]
    for row in range(3):
        table[2 + row : 3 + row, 0:64] = codes[2 * row : 2 * row + 1]
        table[2 + row : 3 + row, 64:128] = codes[2 * row + 1 : 2 * row + 2]
    table[5:6, 0:64] = scale_ref[...].astype(F32)
    columns = jnp.transpose(table[...])
    square = (LANES, LANES)
    first_row = jnp.broadcast_to(table[0:1, :], square).astype(jnp.int32) - me * LANES
    second_row = jnp.broadcast_to(table[1:2, :], square).astype(jnp.int32)
    first_col = jnp.broadcast_to(columns[:, 0:1], square).astype(jnp.int32) - me * LANES
    second_col = jnp.broadcast_to(columns[:, 1:2], square).astype(jnp.int32)

    def onehot(condition):
        return jnp.where(condition, 1.0, 0.0).astype(F32)

    near = onehot(first_col + me * LANES == second_row).astype(BF16)
    near_back = onehot(first_row + me * LANES == second_col).astype(BF16)
    into_faces = onehot(first_row == row_of(square)).astype(BF16)
    peers = (blocks, LANES)
    owner_row = second_row[:blocks] // LANES
    peer_row = row_of(peers)
    to_owner_f = onehot((owner_row == peer_row) & (peer_row != me))
    to_owner = to_owner_f.astype(BF16)
    from_owner = jnp.transpose(to_owner_f).astype(BF16)
    slot_number = (second_row[:blocks] % LANES + 1).astype(F32)
    named = jnp.sum(to_owner_f * slot_number, axis=1, keepdims=True)
    named = jnp.broadcast_to(named, peers)
    for peer in range(blocks):
        named_out[peer] = named[peer : peer + 1, :]

    lane = lane_of((ELEMENTS, LANES))
    low = lane < 64
    node_a, node_b = lane % 64 // 8, lane % 8
    for chunk in range(3):
        code = jnp.where(
            low,
            jnp.broadcast_to(columns[0:64, 2 + chunk : 3 + chunk], lane.shape),
            jnp.broadcast_to(columns[64:128, 2 + chunk : 3 + chunk], lane.shape),
        ).astype(jnp.int32)
        swapped, flip_a, flip_b = code // 4 % 2 == 1, code // 2 % 2 == 1, code % 2 == 1
        half = lane // 64 * 64
        a = jnp.where(flip_a, 7 - node_a, node_a)
        b = jnp.where(flip_b, 7 - node_b, node_b)
        index_to[chunk] = half + jnp.where(swapped, b * 8 + a, a * 8 + b)
        a = jnp.where(swapped, node_b, node_a)
        b = jnp.where(swapped, node_a, node_b)
        index_from[chunk] = half + jnp.where(flip_a, 7 - a, a) * 8 + jnp.where(flip_b, 7 - b, b)
    scales[...] = jnp.broadcast_to(columns[0:64, 5:6], scales.shape)
    live = (low & (layer > 0)) | ((lane >= 64) & (layer < layers - 1))

    def rows_of(right):
        return slice(right * ELEMENTS, (right + 1) * ELEMENTS)

    def lanes_of(chunk):
        return slice(chunk * LANES, (chunk + 1) * LANES)

    loads[0].wait()
    inverse_h[...], inverse_l[...] = halves(inverse[...])
    loads[1].wait()
    coupling_h[...], coupling_l[...] = halves(coupling[...])
    merged = dot_three(inverse_h[...], inverse_l[...], coupling_h[...], coupling_l[...])
    merged_h[...], merged_l[...] = halves(merged)
    loads[2].wait()
    source_h[...], source_l[...] = halves(source[...])
    image[...] = dot_three(source_h[...], source_l[...], merged_h[...], merged_l[...])

    def to_slots(vector, chunks, stores):
        for chunk in chunks:
            for pair in range(PAIRS):
                left = turned(vector[rows_of(2 * pair), lanes_of(chunk)], index_from[chunk])
                right = turned(vector[rows_of(2 * pair + 1), lanes_of(chunk)], index_from[chunk])
                stores[chunk](pair, *swap_pair(left, right))

    def store_slots(ref):
        def store(pair, even, odd):
            ref[0:64, lanes_of(pair)] = even
            ref[64:128, lanes_of(pair)] = odd

        return store

    def store_ends(pair, even, odd):
        bottoms[rows_of(pair), :] = even
        tops[rows_of(pair), :] = odd

    stores = (store_slots(slots_first), store_slots(slots_second), store_ends)

    def all_peers(ref, sem, width):
        whole = ref.at[pl.ds(0, others * width)]
        return pltpu.make_async_copy(whole, whole, sem)

    def up_copy(phase):
        return pltpu.make_async_remote_copy(
            tops,
            got_bottoms.at[phase],
            up_sem.at[phase, 0],
            up_sem.at[phase, 1],
            device_id={"gz": layer + 1},
            device_id_type=MESH,
        )

    def down_copy(phase):
        return pltpu.make_async_remote_copy(
            bottoms,
            got_tops.at[phase],
            down_sem.at[phase, 0],
            down_sem.at[phase, 1],
            device_id={"gz": layer - 1},
            device_id_type=MESH,
        )

    def start_ends(phase):
        @pl.when(layer < layers - 1)
        def _():
            up_copy(phase).start()

        @pl.when(layer > 0)
        def _():
            down_copy(phase).start()

    def finish_ends(phase):
        @pl.when(layer < layers - 1)
        def _():
            up_copy(phase).wait_send()
            down_copy(phase).wait_recv()

        @pl.when(layer > 0)
        def _():
            down_copy(phase).wait_send()
            up_copy(phase).wait_recv()

    def start_swap(phase, to_holder):
        to_owners = pick(to_owner, slots_second[...])
        to_holders = pick(to_holder, slots_first[...])
        for pair in range(PAIRS):
            sent[phase, pl.ds(pair, blocks, stride=8), :] = to_owners[:, lanes_of(pair)]
            sent[phase, pl.ds(pair + 4, blocks, stride=8), :] = to_holders[:, lanes_of(pair)]

        def send(turn, carry):
            peer = partner(me, turn, blocks)
            pltpu.make_async_remote_copy(
                sent.at[phase, pl.ds(pl.multiple_of(peer * 8, 8), 8)],
                received.at[phase, here],
                swap_sem.at[phase, 0],
                swap_sem.at[phase, 1],
                device_id={"dev": peer},
                device_id_type=MESH,
            ).start()
            return carry

        lax.fori_loop(0, others, send, 0)

    def finish_swap(phase, from_holder):
        nearby_first = pick(near, slots_second[...])
        nearby_second = pick(near_back, slots_first[...])
        all_peers(received.at[phase], swap_sem.at[phase, 1], 8).wait()
        all_peers(sent.at[phase], swap_sem.at[phase, 0], 8).wait()
        finish_ends(phase)
        for pair in range(PAIRS):
            from_owners = received[phase, pl.ds(pair + 4, blocks, stride=8), :]
            from_holders = received[phase, pl.ds(pair, blocks, stride=8), :]
            arrived = (
                nearby_first[:, lanes_of(pair)] + pick(from_holder, from_holders),
                nearby_second[:, lanes_of(pair)] + pick(from_owner, from_owners),
                None,
            )
            for chunk in range(3):
                if chunk < 2:
                    even, odd = arrived[chunk][0:64], arrived[chunk][64:128]
                else:
                    even, odd = got_bottoms[phase, rows_of(pair), :], got_tops[phase, rows_of(pair), :]
                for offset, value in enumerate(swap_pair(even, odd)):
                    yield 2 * pair + offset, chunk, turned(value, index_to[chunk])

    def start_sum(phase, quantities):
        lanes = lane_of((RIGHT, LANES))
        place = row_of((RIGHT, LANES))
        spread = jnp.zeros((RIGHT, LANES), F32)
        for number, rows in enumerate(quantities):
            total = jnp.sum(jnp.concatenate(rows, axis=0), axis=1, keepdims=True)
            spread = jnp.where(lanes == place + number * RIGHT, total, spread)
        mine = jnp.sum(spread, axis=0, keepdims=True)
        sum_out[phase] = mine
        sum_in[phase, me] = mine

        def send(turn, carry):
            pltpu.make_async_remote_copy(
                sum_out.at[phase],
                sum_in.at[phase, me],
                sum_sem.at[phase, 0],
                sum_sem.at[phase, 1],
                device_id={"dev": partner(me, turn, blocks)},
                device_id_type=MESH,
            ).start()
            return carry

        lax.fori_loop(0, others, send, 0)

    def finish_sum(phase, count):
        all_peers(sum_in.at[phase], sum_sem.at[phase, 1], 1).wait()
        all_peers(sum_in.at[phase], sum_sem.at[phase, 0], 1).wait()
        mine = jnp.sum(sum_in[phase], axis=0)
        layer_out[phase] = mine
        layer_in[phase, layer] = mine
        for step in range(1, layers):
            pltpu.make_async_remote_copy(
                layer_out.at[phase],
                layer_in.at[phase, layer],
                layer_sem.at[phase, 0],
                layer_sem.at[phase, 1],
                device_id={"gz": (layer + step) % layers},
                device_id_type=MESH,
            ).start()
        rest = layer_in.at[phase, pl.ds(0, layers - 1)]
        pltpu.make_async_copy(rest, rest, layer_sem.at[phase, 1]).wait()
        pltpu.make_async_copy(rest, rest, layer_sem.at[phase, 0]).wait()
        total = jnp.broadcast_to(jnp.sum(layer_in[phase], axis=0), (RIGHT, LANES))
        lanes = lane_of((RIGHT, LANES))
        place = row_of((RIGHT, LANES))
        return [
            jnp.broadcast_to(
                jnp.sum(
                    jnp.where(lanes == place + number * RIGHT, total, 0.0), axis=1, keepdims=True
                ),
                (RIGHT, LANES),
            )
            for number in range(count)
        ]

    def owned_square(values):
        kept = values[0] * values[0] + jnp.where(low, 0.0, values[2] * values[2])
        return jnp.sum(kept, axis=0, keepdims=True)

    def inner_rows(left, right):
        kept = left[0] * right[0] + left[1] * right[1] + left[2] * right[2]
        return jnp.sum(kept, axis=0, keepdims=True)

    def chunks_of(ref, right):
        return [ref[rows_of(right), lanes_of(chunk)] for chunk in range(3)]

    def scaled_operator():
        return dot_three(vector_h[...], vector_l[...], operator_h[...], operator_l[...])

    def face_values(vector, sides_ref, tops_ref):
        for pair in range(PAIRS):
            for chunk in (0, 2):
                left = turned(vector[rows_of(2 * pair), lanes_of(chunk)], index_from[chunk])
                right = turned(vector[rows_of(2 * pair + 1), lanes_of(chunk)], index_from[chunk])
                even, odd = swap_pair(left, right)
                if chunk == 0:
                    turned_back = jnp.transpose(
                        pick(into_faces, jnp.concatenate([even, odd], axis=0))
                    )
                    target = sides_ref
                else:
                    turned_back = jnp.transpose(odd)
                    target = tops_ref
                for offset in range(2):
                    target[pl.ds(2 * pair + offset, 64, stride=8), :] = turned_back[
                        offset * 64 : (offset + 1) * 64
                    ]

    to_slots(image, (2, 1, 0), stores)
    pl.semaphore_wait(barrier, others + layers - 1)

    def name(turn, carry):
        peer = partner(me, turn, blocks)
        pltpu.make_async_remote_copy(
            named_out.at[peer],
            named_in.at[me],
            named_sem.at[0],
            named_sem.at[1],
            device_id={"dev": peer},
            device_id_type=MESH,
        ).start()
        return carry

    lax.fori_loop(0, others, name, 0)
    start_ends(0)
    solved[...] = dot_three(source_h[...], source_l[...], inverse_h[...], inverse_l[...])
    loads[3].wait()
    operator_h[...], operator_l[...] = halves(operator[...])
    all_peers(named_in, named_sem.at[1], 1).wait()
    all_peers(named_out, named_sem.at[0], 1).wait()
    wanted = named_in[...].reshape(blocks, LANES)
    to_holder_f = onehot(wanted.astype(jnp.int32) == first_row[:blocks] + 1)
    to_holder = to_holder_f.astype(BF16)
    from_holder = jnp.transpose(to_holder_f).astype(BF16)
    start_swap(0, to_holder)

    for right in range(RIGHT):
        for part in range(4):
            solved[rows_of(right), lanes_of(part)] = solved[rows_of(right), lanes_of(part)] / scales[...]
    merged_th[...] = jnp.transpose(merged_h[...].astype(F32)).astype(BF16)
    merged_tl[...] = jnp.transpose(merged_l[...].astype(F32)).astype(BF16)

    for right, chunk, value in finish_swap(0, from_holder):
        value = image[rows_of(right), lanes_of(chunk)] + value
        if chunk == 2:
            value = jnp.where(live, value, 0.0)
        first[rows_of(right), lanes_of(chunk)] = value
        vector_h[rows_of(right), lanes_of(chunk)], vector_l[rows_of(right), lanes_of(chunk)] = halves(value)

    image[...] = scaled_operator()
    squares, curves = [], []
    for right in range(RIGHT):
        for chunk in range(3):
            image[rows_of(right), lanes_of(chunk)] = image[rows_of(right), lanes_of(chunk)] * scales[...]
        mine = chunks_of(first, right)
        squares.append(owned_square(mine))
        curves.append(inner_rows(mine, chunks_of(image, right)))
    start_sum(0, [squares, curves])
    to_slots(image, (2, 1, 0), stores)
    start_ends(1)
    start_swap(1, to_holder)

    moved_zero[...] = dot_three(vector_h[...], vector_l[...], merged_th[...], merged_tl[...])
    face_values(first, sides_zero, tops_zero)
    norm, curve = finish_sum(0, 2)
    alpha = norm / curve

    for right, chunk, value in finish_swap(1, from_holder):
        value = image[rows_of(right), lanes_of(chunk)] + value
        value = first[rows_of(right), lanes_of(chunk)] - alpha[right : right + 1, :] * value
        if chunk == 2:
            value = jnp.where(live, value, 0.0)
        update[rows_of(right), lanes_of(chunk)] = value
        vector_h[rows_of(right), lanes_of(chunk)], vector_l[rows_of(right), lanes_of(chunk)] = halves(value)

    second_image = scaled_operator()
    squares, crosses, curves = [], [], []
    for right in range(RIGHT):
        mine = chunks_of(update, right)
        squares.append(owned_square(mine))
        crosses.append(inner_rows(mine, chunks_of(image, right)))
        scaled = [second_image[rows_of(right), lanes_of(chunk)] * scales[...] for chunk in range(3)]
        curves.append(inner_rows(mine, scaled))
    start_sum(1, [squares, crosses, curves])

    moved_one[...] = dot_three(vector_h[...], vector_l[...], merged_th[...], merged_tl[...])
    face_values(update, sides_one, tops_one)
    norm_next, cross, curve_next = finish_sum(1, 3)
    beta = norm_next / norm
    curve_next = curve_next + 2.0 * beta * cross + beta * beta * curve
    weight_one = norm_next / curve_next
    weight_zero = alpha + weight_one * beta

    writes = []
    for right in range(RIGHT):
        for part in range(4):
            spot = rows_of(right), lanes_of(part)
            solved[spot] = (
                solved[spot]
                - weight_zero[right : right + 1, :] * moved_zero[spot]
                - weight_one[right : right + 1, :] * moved_one[spot]
            )
    writes.append(pltpu.make_async_copy(solved, interior_hbm, store_sem.at[0]))
    writes[-1].start()
    for node in range(64):
        spot = slice(node * 8, node * 8 + 8)
        sides_zero[spot, :] = weight_zero * sides_zero[spot, :] + weight_one * sides_one[spot, :]
        tops_zero[spot, :] = weight_zero[:, :64] * tops_zero[spot, :] + weight_one[:, :64] * tops_one[spot, :]
    writes.append(pltpu.make_async_copy(sides_zero, sides_hbm, store_sem.at[1]))
    writes[-1].start()
    writes.append(pltpu.make_async_copy(tops_zero, tops_hbm, store_sem.at[2]))
    writes[-1].start()
    for write in writes:
        write.wait()


def solution(mesh):
    layers, blocks = mesh.shape["gz"], mesh.shape["dev"]

    def per_device(source, inverse, coupling, operator, face_ids, orientation, scale):
        flat = source.transpose(1, 2, 0).reshape(ROWS, NODES)
        vmem = pltpu.VMEM
        anywhere = pl.BlockSpec(memory_space=pl.ANY)
        local = pl.BlockSpec(memory_space=pltpu.VMEM)
        dma = pltpu.SemaphoreType.DMA
        interior, sides, tops = pl.pallas_call(
            functools.partial(kernel, layers, blocks),
            out_shape=(
                jax.ShapeDtypeStruct((ROWS, NODES), F32),
                jax.ShapeDtypeStruct((512, 128), F32),
                jax.ShapeDtypeStruct((512, 64), F32),
            ),
            in_specs=[anywhere] * 4 + [local] * 3,
            out_specs=(anywhere,) * 3,
            scratch_shapes=[
                vmem((ROWS, NODES), F32),
                vmem((NODES, NODES), F32),
                vmem((NODES, LOCAL), F32),
                vmem((LOCAL, LOCAL), F32),
                *[vmem((ROWS, NODES), BF16)] * 2,
                *[vmem((NODES, NODES), BF16)] * 2,
                *[vmem((NODES, LOCAL), BF16)] * 2,
                *[vmem((LOCAL, LOCAL), BF16)] * 2,
                *[vmem((NODES, LOCAL), BF16)] * 2,
                *[vmem((LOCAL, NODES), BF16)] * 2,
                vmem((LANES, LANES), F32),
                vmem((3, ELEMENTS, LANES), jnp.int32),
                vmem((3, ELEMENTS, LANES), jnp.int32),
                vmem((ELEMENTS, LANES), F32),
                *[vmem((ROWS, LOCAL), F32)] * 3,
                *[vmem((ROWS, LOCAL), BF16)] * 2,
                *[vmem((128, 512), F32)] * 2,
                *[vmem((256, 128), F32)] * 2,
                *[vmem((ROWS, NODES), F32)] * 3,
                *[vmem((512, 128), F32)] * 2,
                *[vmem((512, 64), F32)] * 2,
                *[vmem((blocks, 1, LANES), F32)] * 2,
                *[vmem((2, blocks * 8, LANES), F32)] * 2,
                *[vmem((2, 256, 128), F32)] * 2,
                vmem((2, 1, LANES), F32),
                vmem((2, blocks, 1, LANES), F32),
                vmem((2, 1, LANES), F32),
                vmem((2, layers, 1, LANES), F32),
                dma((4,)),
                dma((3,)),
                dma((2,)),
                dma((2, 2)),
                dma((2, 2)),
                dma((2, 2)),
                dma((2, 2)),
                dma((2, 2)),
            ],
            compiler_params=pltpu.CompilerParams(collective_id=0, has_side_effects=True),
        )(
            flat,
            inverse,
            coupling,
            operator,
            face_ids.T,
            orientation.T,
            scale.reshape(1, ELEMENTS),
        )
        return (
            interior.reshape(RIGHT, ELEMENTS, NODES).transpose(2, 0, 1),
            sides.reshape(64, RIGHT, 128),
            tops.reshape(64, RIGHT, ELEMENTS),
        )

    columns = P(None, None, ("gz", "dev"))
    return jax.shard_map(
        per_device,
        mesh=mesh,
        in_specs=(
            columns,
            P(),
            P(),
            P(),
            P(("gz", "dev"), None),
            P(("gz", "dev"), None),
            P(("gz", "dev")),
        ),
        out_specs=(columns, columns, columns),
        check_vma=False,
    )
```

```python
import functools

import jax
import jax.numpy as jnp
from jax import lax
from jax.experimental import pallas as pl
from jax.experimental.pallas import tpu as pltpu
from jax.sharding import PartitionSpec as P

MESH = pl.DeviceIdType.MESH
F32 = jnp.float32
BF16 = jnp.bfloat16
LANES = 128
ELEMENTS = 64
RIGHT = 8
NODES = 512
LOCAL = 384
ROWS = RIGHT * ELEMENTS
PAIRS = RIGHT // 2


def partner(me, turn, count):
    if count != 64:
        return (me + 1 + turn) % count
    far_z, far_y, far_core = turn // 8, turn % 8 // 2, turn % 2
    step_z = (4 + (far_z + 1) // 2 * (1 - 2 * (far_z % 2))) % 8
    step_y = (2 + (far_y + 1) // 2 * (1 - 2 * (far_y % 2))) % 4
    z = (me // 8 + step_z) % 8
    y = (me % 8 // 2 + step_y) % 4
    core = (me % 2 + 1 - far_core) % 2
    return z * 8 + y * 2 + core


def halves(value):
    high = value.astype(BF16)
    return high, (value - high.astype(F32)).astype(BF16)


def dot(left, right):
    return jnp.dot(left, right, preferred_element_type=F32)


def dot_three(left_high, left_low, right_high, right_low):
    return dot(left_high, right_high) + (dot(left_high, right_low) + dot(left_low, right_high))


def pick(onehot, value):
    high, low = halves(value)
    return dot(onehot, high) + dot(onehot, low)


def lane_of(shape):
    return lax.broadcasted_iota(jnp.int32, shape, 1)


def row_of(shape):
    return lax.broadcasted_iota(jnp.int32, shape, 0)


def swap_pair(first, second):
    low = lane_of(first.shape) < 64
    return (
        jnp.where(low, first, pltpu.roll(second, 64, 1)),
        jnp.where(low, pltpu.roll(first, 64, 1), second),
    )


def turned(value, index):
    return jnp.take_along_axis(value, index, axis=1, mode="promise_in_bounds")


def kernel(
    layers,
    blocks,
    source_hbm,
    inverse_hbm,
    coupling_hbm,
    operator_hbm,
    faces_hbm,
    codes_hbm,
    scale_hbm,
    solved,
    moved_zero,
    moved_one,
    sides_zero,
    sides_one,
    tops_zero,
    tops_one,
    weights,
    source,
    inverse,
    coupling,
    operator,
    faces_ref,
    codes_ref,
    scale_ref,
    source_h,
    source_l,
    inverse_h,
    inverse_l,
    coupling_h,
    coupling_l,
    operator_h,
    operator_l,
    merged_h,
    merged_l,
    merged_th,
    merged_tl,
    table,
    index_to,
    index_from,
    scales,
    first,
    image,
    update,
    vector_h,
    vector_l,
    slots_first,
    slots_second,
    bottoms,
    tops,
    second_image,
    sent,
    received,
    got_bottoms,
    got_tops,
    near_out,
    near_in,
    far_out,
    far_in,
    load_sem,
    swap_sem,
    up_sem,
    down_sem,
    near_sem,
    far_sem,
):
    layer = lax.axis_index("gz")
    me = lax.axis_index("dev")
    others = blocks - 1
    core = me % 2
    core_pair = me // 2 * 2

    barrier = pltpu.get_barrier_semaphore()

    def greet(turn, carry):
        pl.semaphore_signal(
            barrier, inc=1, device_id={"dev": partner(me, turn, blocks)}, device_id_type=MESH
        )
        return carry

    lax.fori_loop(0, others, greet, 0)
    for step in range(1, layers):
        for side in range(2):
            pl.semaphore_signal(
                barrier,
                inc=1,
                device_id=((layer + step) % layers, core_pair + (core + side) % 2),
                device_id_type=MESH,
            )

    loads = [
        pltpu.make_async_copy(inverse_hbm, inverse, load_sem.at[0]),
        pltpu.make_async_copy(coupling_hbm, coupling, load_sem.at[1]),
        pltpu.make_async_copy(source_hbm, source, load_sem.at[2]),
        pltpu.make_async_copy(operator_hbm, operator, load_sem.at[3]),
        pltpu.make_async_copy(faces_hbm, faces_ref, load_sem.at[4]),
        pltpu.make_async_copy(codes_hbm, codes_ref, load_sem.at[5]),
        pltpu.make_async_copy(scale_hbm, scale_ref, load_sem.at[6]),
    ]
    for load in loads[4:] + loads[:4]:
        load.start()

    here = pl.ds(pl.multiple_of(me * 8, 8), 8)
    for phase in range(3):
        received[phase, here, :] = jnp.zeros((8, LANES), F32)

    @pl.when(layer == 0)
    def _():
        got_bottoms[...] = jnp.zeros(got_bottoms.shape, F32)

    @pl.when(layer == layers - 1)
    def _():
        got_tops[...] = jnp.zeros(got_tops.shape, F32)

    table[...] = jnp.zeros(table.shape, F32)
    for load in loads[4:]:
        load.wait()
    faces = faces_ref[...].astype(F32)
    codes = codes_ref[...].astype(F32)
    for row in range(2):
        table[row : row + 1, 0:64] = faces[2 * row : 2 * row + 1]
        table[row : row + 1, 64:128] = faces[2 * row + 1 : 2 * row + 2]
    for row in range(3):
        table[2 + row : 3 + row, 0:64] = codes[2 * row : 2 * row + 1]
        table[2 + row : 3 + row, 64:128] = codes[2 * row + 1 : 2 * row + 2]
    table[5:6, 0:64] = scale_ref[...].astype(F32)
    columns = jnp.transpose(table[...])
    square = (LANES, LANES)
    first_row = jnp.broadcast_to(table[0:1, :], square).astype(jnp.int32) - me * LANES
    second_row = jnp.broadcast_to(table[1:2, :], square).astype(jnp.int32)
    first_col = jnp.broadcast_to(columns[:, 0:1], square).astype(jnp.int32) - me * LANES
    second_col = jnp.broadcast_to(columns[:, 1:2], square).astype(jnp.int32)

    def onehot(condition):
        return jnp.where(condition, 1.0, 0.0).astype(F32)

    near = onehot(first_col + me * LANES == second_row).astype(BF16)
    near_back = onehot(first_row + me * LANES == second_col).astype(BF16)
    into_faces = onehot(first_row == row_of(square)).astype(BF16)
    peers = (blocks, LANES)
    owner_row = second_row[:blocks] // LANES
    peer_row = row_of(peers)
    to_owner_f = onehot((owner_row == peer_row) & (peer_row != me))
    to_owner = to_owner_f.astype(BF16)
    from_owner = jnp.transpose(to_owner_f).astype(BF16)
    slot_number = (second_row[:blocks] % LANES + 1).astype(F32)
    named = jnp.sum(to_owner_f * slot_number, axis=1, keepdims=True)
    sent[0, pl.ds(4, blocks, stride=8), :] = jnp.broadcast_to(named, peers)

    lane = lane_of((ELEMENTS, LANES))
    low = lane < 64
    node_a, node_b = lane % 64 // 8, lane % 8
    for chunk in range(3):
        code = jnp.where(
            low,
            jnp.broadcast_to(columns[0:64, 2 + chunk : 3 + chunk], lane.shape),
            jnp.broadcast_to(columns[64:128, 2 + chunk : 3 + chunk], lane.shape),
        ).astype(jnp.int32)
        swapped, flip_a, flip_b = code // 4 % 2 == 1, code // 2 % 2 == 1, code % 2 == 1
        half = lane // 64 * 64
        a = jnp.where(flip_a, 7 - node_a, node_a)
        b = jnp.where(flip_b, 7 - node_b, node_b)
        index_to[chunk] = half + jnp.where(swapped, b * 8 + a, a * 8 + b)
        a = jnp.where(swapped, node_b, node_a)
        b = jnp.where(swapped, node_a, node_b)
        index_from[chunk] = half + jnp.where(flip_a, 7 - a, a) * 8 + jnp.where(flip_b, 7 - b, b)
    scales[...] = jnp.broadcast_to(columns[0:64, 5:6], scales.shape)
    live = (low & (layer > 0)) | ((lane >= 64) & (layer < layers - 1))

    def rows_of(right):
        return slice(right * ELEMENTS, (right + 1) * ELEMENTS)

    def lanes_of(chunk):
        return slice(chunk * LANES, (chunk + 1) * LANES)

    loads[0].wait()
    inverse_h[...], inverse_l[...] = halves(inverse[...])
    loads[1].wait()
    coupling_h[...], coupling_l[...] = halves(coupling[...])
    merged = dot_three(inverse_h[...], inverse_l[...], coupling_h[...], coupling_l[...])
    merged_h[...], merged_l[...] = halves(merged)
    loads[2].wait()
    source_h[...], source_l[...] = halves(source[...])
    image[...] = dot_three(source_h[...], source_l[...], merged_h[...], merged_l[...])

    def to_slots(vector, chunks, stores):
        for chunk in chunks:
            for pair in range(PAIRS):
                left = turned(vector[rows_of(2 * pair), lanes_of(chunk)], index_from[chunk])
                right = turned(vector[rows_of(2 * pair + 1), lanes_of(chunk)], index_from[chunk])
                stores[chunk](pair, *swap_pair(left, right))

    def store_slots(ref):
        def store(pair, even, odd):
            ref[0:64, lanes_of(pair)] = even
            ref[64:128, lanes_of(pair)] = odd

        return store

    def store_ends(pair, even, odd):
        bottoms[rows_of(pair), :] = even
        tops[rows_of(pair), :] = odd

    stores = (store_slots(slots_first), store_slots(slots_second), store_ends)

    def wait_rows(ref, rows, sem):
        whole = ref.at[pl.ds(0, rows)]
        pltpu.make_async_copy(whole, whole, sem).wait()

    def up_copy(phase):
        return pltpu.make_async_remote_copy(
            tops,
            got_bottoms.at[phase],
            up_sem.at[phase, 0],
            up_sem.at[phase, 1],
            device_id={"gz": layer + 1},
            device_id_type=MESH,
        )

    def down_copy(phase):
        return pltpu.make_async_remote_copy(
            bottoms,
            got_tops.at[phase],
            down_sem.at[phase, 0],
            down_sem.at[phase, 1],
            device_id={"gz": layer - 1},
            device_id_type=MESH,
        )

    def start_ends(phase):
        @pl.when(layer < layers - 1)
        def _():
            up_copy(phase).start()

        @pl.when(layer > 0)
        def _():
            down_copy(phase).start()

    def finish_ends(phase):
        @pl.when(layer < layers - 1)
        def _():
            up_copy(phase).wait_send()
            down_copy(phase).wait_recv()

        @pl.when(layer > 0)
        def _():
            down_copy(phase).wait_send()
            up_copy(phase).wait_recv()

    def send_rows(phase, rows):
        def send(turn, carry):
            peer = partner(me, turn, blocks)
            pltpu.make_async_remote_copy(
                sent.at[phase, pl.ds(pl.multiple_of(peer * 8, 8), rows)],
                received.at[phase, pl.ds(pl.multiple_of(me * 8, 8), rows)],
                swap_sem.at[phase, 0],
                swap_sem.at[phase, 1],
                device_id={"dev": peer},
                device_id_type=MESH,
            ).start()
            return carry

        lax.fori_loop(0, others, send, 0)

    def wait_sent(phase, rows):
        wait_rows(sent.at[phase], others * rows, swap_sem.at[phase, 0])

    def wait_received(phase, rows):
        wait_rows(received.at[phase], others * rows, swap_sem.at[phase, 1])

    def put(phase, first_row, value):
        for pair in range(PAIRS):
            sent[phase, pl.ds(first_row + pair, blocks, stride=8), :] = value[:, lanes_of(pair)]

    def got(phase, row):
        return received[phase, pl.ds(row, blocks, stride=8), :]

    def arrivals(chunk, pair, value):
        for offset, part in enumerate(swap_pair(value[0:64], value[64:128])):
            yield 2 * pair + offset, turned(part, index_to[chunk])

    def end_arrivals(phase):
        for pair in range(PAIRS):
            ends = got_bottoms[phase, rows_of(pair), :], got_tops[phase, rows_of(pair), :]
            for right, part in arrivals(2, pair, jnp.concatenate(ends, axis=0)):
                spot = rows_of(right), lanes_of(2)
                yield spot, jnp.where(live, image[spot] + part, 0.0)

    def keep(ref, spot, value):
        ref[spot] = value
        vector_h[spot], vector_l[spot] = halves(value)

    def sum_peer(turn):
        step = (layers // 2 + (turn // 2 + 1) // 2 * (1 - 2 * (turn // 2 % 2))) % layers
        return (layer + step) % layers, core_pair + (core + 1 - turn % 2) % 2

    def far_peer(turn):
        if blocks == 64:
            return partner(me, 2 * turn + 1, blocks)
        return (me + 2 * (turn + 1)) % blocks

    def start_sum(phase, quantities):
        lanes = lane_of((RIGHT, LANES))
        place = row_of((RIGHT, LANES))
        spread = jnp.zeros((RIGHT, LANES), F32)
        for number, rows in enumerate(quantities):
            total = jnp.sum(jnp.concatenate(rows, axis=0), axis=1, keepdims=True)
            spread = jnp.where(lanes == place + number * RIGHT, total, spread)
        mine = jnp.sum(spread, axis=0, keepdims=True)
        near_out[phase] = mine
        near_in[phase, layer * 2 + core] = mine

        def send(turn, carry):
            pltpu.make_async_remote_copy(
                near_out.at[phase],
                near_in.at[phase, layer * 2 + core],
                near_sem.at[phase, 0],
                near_sem.at[phase, 1],
                device_id=sum_peer(turn),
                device_id_type=MESH,
            ).start()
            return carry

        lax.fori_loop(0, 2 * layers - 1, send, 0)

    def middle_sum(phase):
        wait_rows(near_in.at[phase], 2 * layers - 1, near_sem.at[phase, 1])
        wait_rows(near_in.at[phase], 2 * layers - 1, near_sem.at[phase, 0])
        mine = jnp.sum(near_in[phase], axis=0)
        far_out[phase] = mine
        far_in[phase, me // 2] = mine

        def send(turn, carry):
            pltpu.make_async_remote_copy(
                far_out.at[phase],
                far_in.at[phase, me // 2],
                far_sem.at[phase, 0],
                far_sem.at[phase, 1],
                device_id={"dev": far_peer(turn)},
                device_id_type=MESH,
            ).start()
            return carry

        lax.fori_loop(0, blocks // 2 - 1, send, 0)

    def finish_sum(phase, count):
        wait_rows(far_in.at[phase], blocks // 2 - 1, far_sem.at[phase, 1])
        wait_rows(far_in.at[phase], blocks // 2 - 1, far_sem.at[phase, 0])
        total = jnp.broadcast_to(jnp.sum(far_in[phase], axis=0), (RIGHT, LANES))
        lanes = lane_of((RIGHT, LANES))
        place = row_of((RIGHT, LANES))
        return [
            jnp.broadcast_to(
                jnp.sum(
                    jnp.where(lanes == place + number * RIGHT, total, 0.0), axis=1, keepdims=True
                ),
                (RIGHT, LANES),
            )
            for number in range(count)
        ]

    def owned_square(values):
        kept = values[0] * values[0] + jnp.where(low, 0.0, values[2] * values[2])
        return jnp.sum(kept, axis=0, keepdims=True)

    def inner_rows(left, right):
        kept = left[0] * right[0] + left[1] * right[1] + left[2] * right[2]
        return jnp.sum(kept, axis=0, keepdims=True)

    def chunks_of(ref, right):
        return [ref[rows_of(right), lanes_of(chunk)] for chunk in range(3)]

    def operated(chunks):
        return sum(
            dot_three(
                vector_h[:, lanes_of(chunk)],
                vector_l[:, lanes_of(chunk)],
                operator_h[lanes_of(chunk), :],
                operator_l[lanes_of(chunk), :],
            )
            for chunk in chunks
        )

    def face_values(vector, sides_ref, tops_ref):
        for pair in range(PAIRS):
            for chunk in (0, 2):
                left = turned(vector[rows_of(2 * pair), lanes_of(chunk)], index_from[chunk])
                right = turned(vector[rows_of(2 * pair + 1), lanes_of(chunk)], index_from[chunk])
                even, odd = swap_pair(left, right)
                if chunk == 0:
                    turned_back = jnp.transpose(
                        pick(into_faces, jnp.concatenate([even, odd], axis=0))
                    )
                    target = sides_ref
                else:
                    turned_back = jnp.transpose(odd)
                    target = tops_ref
                for offset in range(2):
                    target[pl.ds(2 * pair + offset, 64, stride=8), :] = turned_back[
                        offset * 64 : (offset + 1) * 64
                    ]

    to_slots(image, (2, 1, 0), stores)
    put(0, 0, pick(to_owner, slots_second[...]))
    pl.semaphore_wait(barrier, others + 2 * (layers - 1))

    send_rows(0, 5)
    start_ends(0)
    solved[...] = dot_three(source_h[...], source_l[...], inverse_h[...], inverse_l[...])
    loads[3].wait()
    operator_h[...], operator_l[...] = halves(operator[...])
    nearby_first = pick(near, slots_second[...])
    wait_received(0, 5)
    to_holder_f = onehot(got(0, 4).astype(jnp.int32) == first_row[:blocks] + 1)
    to_holder = to_holder_f.astype(BF16)
    from_holder = jnp.transpose(to_holder_f).astype(BF16)

    put(1, 0, pick(to_holder, slots_first[...]))
    send_rows(1, 4)
    for pair in range(PAIRS):
        value = nearby_first[:, lanes_of(pair)] + pick(from_holder, got(0, pair))
        for right, part in arrivals(0, pair, value):
            spot = rows_of(right), lanes_of(0)
            keep(first, spot, image[spot] + part)
    finish_ends(0)
    for spot, value in end_arrivals(0):
        keep(first, spot, value)
    second_image[...] = operated((0, 2))
    nearby_second = pick(near_back, slots_first[...])
    wait_received(1, 4)
    for pair in range(PAIRS):
        value = nearby_second[:, lanes_of(pair)] + pick(from_owner, got(1, pair))
        for right, part in arrivals(1, pair, value):
            spot = rows_of(right), lanes_of(1)
            keep(first, spot, image[spot] + part)
    image[...] = second_image[...] + operated((1,))

    squares, curves = [], []
    for right in range(RIGHT):
        for chunk in range(3):
            image[rows_of(right), lanes_of(chunk)] = image[rows_of(right), lanes_of(chunk)] * scales[...]
        mine = chunks_of(first, right)
        squares.append(owned_square(mine))
        curves.append(inner_rows(mine, chunks_of(image, right)))
    start_sum(0, [squares, curves])
    wait_sent(0, 5)
    wait_sent(1, 4)
    to_slots(image, (1, 0, 2), stores)
    put(2, 0, pick(to_owner, slots_second[...]))
    put(2, 4, pick(to_holder, slots_first[...]))
    send_rows(2, 8)
    start_ends(1)

    middle_sum(0)
    nearby_first = pick(near, slots_second[...])
    nearby_second = pick(near_back, slots_first[...])
    for right in range(RIGHT):
        for part in range(4):
            solved[rows_of(right), lanes_of(part)] = solved[rows_of(right), lanes_of(part)] / scales[...]
    merged_th[...] = jnp.transpose(merged_h[...].astype(F32)).astype(BF16)
    merged_tl[...] = jnp.transpose(merged_l[...].astype(F32)).astype(BF16)
    moved_zero[...] = dot_three(vector_h[...], vector_l[...], merged_th[...], merged_tl[...])
    face_values(first, sides_zero, tops_zero)
    finish_ends(1)
    for spot, value in end_arrivals(1):
        keep(update, spot, value)
    wait_received(2, 8)
    wait_sent(2, 8)
    for pair in range(PAIRS):
        arrived = (
            nearby_first[:, lanes_of(pair)] + pick(from_holder, got(2, pair)),
            nearby_second[:, lanes_of(pair)] + pick(from_owner, got(2, pair + 4)),
        )
        for chunk in range(2):
            for right, part in arrivals(chunk, pair, arrived[chunk]):
                spot = rows_of(right), lanes_of(chunk)
                keep(update, spot, image[spot] + part)
    second_image[...] = operated((0, 1, 2))

    norm, curve = finish_sum(0, 2)
    alpha = norm / curve
    squares, crosses, curves = [], [], []
    for right in range(RIGHT):
        step = alpha[right : right + 1, :]
        before, change = chunks_of(first, right), chunks_of(update, right)
        old, turned_change = chunks_of(image, right), chunks_of(second_image, right)
        mine = [before[chunk] - step * change[chunk] for chunk in range(3)]
        new = [old[chunk] - step * (turned_change[chunk] * scales[...]) for chunk in range(3)]
        squares.append(owned_square(mine))
        crosses.append(inner_rows(mine, old))
        curves.append(inner_rows(mine, new))
    start_sum(1, [squares, crosses, curves])

    moved_one[...] = dot_three(vector_h[...], vector_l[...], merged_th[...], merged_tl[...])
    middle_sum(1)
    face_values(update, sides_one, tops_one)
    norm_next, cross, curve_next = finish_sum(1, 3)
    beta = norm_next / norm
    curve_next = curve_next + 2.0 * beta * cross + beta * beta * curve
    weight_update = norm_next / curve_next
    weights[0:8, :] = alpha + weight_update * beta + weight_update
    weights[8:16, :] = weight_update * alpha


def combine(weights, solved, moved_zero, moved_one, sides_zero, sides_one, tops_zero, tops_one, interior, sides, tops):
    for right in range(RIGHT):
        for part in range(4):
            spot = slice(right * 64, right * 64 + 64), slice(part * LANES, part * LANES + LANES)
            interior[spot] = (
                solved[spot]
                - weights[right : right + 1, :] * moved_zero[spot]
                + weights[8 + right : 9 + right, :] * moved_one[spot]
            )
    for node in range(64):
        spot = slice(node * 8, node * 8 + 8)
        sides[spot, :] = weights[0:8, :] * sides_zero[spot, :] - weights[8:16, :] * sides_one[spot, :]
        tops[spot, :] = weights[0:8, :64] * tops_zero[spot, :] - weights[8:16, :64] * tops_one[spot, :]


def solution(mesh):
    layers, blocks = mesh.shape["gz"], mesh.shape["dev"]

    def per_device(source, inverse, coupling, operator, face_ids, orientation, scale):
        flat = source.transpose(1, 2, 0).reshape(ROWS, NODES)
        vmem = pltpu.VMEM
        far = pl.BlockSpec(memory_space=pltpu.HBM)
        local = pl.BlockSpec(memory_space=pltpu.VMEM)
        dma = pltpu.SemaphoreType.DMA
        shapes = [
            *[jax.ShapeDtypeStruct((ROWS, NODES), F32)] * 3,
            *[jax.ShapeDtypeStruct((512, 128), F32)] * 2,
            *[jax.ShapeDtypeStruct((512, 64), F32)] * 2,
            jax.ShapeDtypeStruct((16, LANES), F32),
        ]
        *found, weights = pl.pallas_call(
            functools.partial(kernel, layers, blocks),
            out_shape=tuple(shapes),
            in_specs=[far] * 7,
            out_specs=(local,) * 8,
            scratch_shapes=[
                vmem((ROWS, NODES), F32),
                vmem((NODES, NODES), F32),
                vmem((NODES, LOCAL), F32),
                vmem((LOCAL, LOCAL), F32),
                vmem((4, ELEMENTS), jnp.int32),
                vmem((6, ELEMENTS), jnp.int32),
                vmem((1, ELEMENTS), jnp.int32),
                *[vmem((ROWS, NODES), BF16)] * 2,
                *[vmem((NODES, NODES), BF16)] * 2,
                *[vmem((NODES, LOCAL), BF16)] * 2,
                *[vmem((LOCAL, LOCAL), BF16)] * 2,
                *[vmem((NODES, LOCAL), BF16)] * 2,
                *[vmem((LOCAL, NODES), BF16)] * 2,
                vmem((LANES, LANES), F32),
                vmem((3, ELEMENTS, LANES), jnp.int32),
                vmem((3, ELEMENTS, LANES), jnp.int32),
                vmem((ELEMENTS, LANES), F32),
                *[vmem((ROWS, LOCAL), F32)] * 3,
                *[vmem((ROWS, LOCAL), BF16)] * 2,
                *[vmem((128, 512), F32)] * 2,
                *[vmem((256, 128), F32)] * 2,
                vmem((ROWS, LOCAL), F32),
                *[vmem((3, blocks * 8, LANES), F32)] * 2,
                *[vmem((2, 256, 128), F32)] * 2,
                vmem((2, 1, LANES), F32),
                vmem((2, 2 * layers, 1, LANES), F32),
                vmem((2, 1, LANES), F32),
                vmem((2, blocks // 2, 1, LANES), F32),
                dma((7,)),
                dma((3, 2)),
                dma((2, 2)),
                dma((2, 2)),
                dma((2, 2)),
                dma((2, 2)),
            ],
            compiler_params=pltpu.CompilerParams(
                collective_id=0, has_side_effects=True, vmem_limit_bytes=32 << 20
            ),
        )(
            flat,
            inverse,
            coupling,
            operator,
            face_ids.T,
            orientation.T,
            scale.reshape(1, ELEMENTS),
        )
        interior, sides, tops = pl.pallas_call(
            combine,
            out_shape=(shapes[0], shapes[3], shapes[5]),
            in_specs=[local] * 8,
            out_specs=(local,) * 3,
            compiler_params=pltpu.CompilerParams(vmem_limit_bytes=16 << 20),
        )(weights, *found)
        return (
            interior.reshape(RIGHT, ELEMENTS, NODES).transpose(2, 0, 1),
            sides.reshape(64, RIGHT, 128),
            tops.reshape(64, RIGHT, ELEMENTS),
        )

    columns = P(None, None, ("gz", "dev"))
    return jax.shard_map(
        per_device,
        mesh=mesh,
        in_specs=(
            columns,
            P(),
            P(),
            P(),
            P(("gz", "dev"), None),
            P(("gz", "dev"), None),
            P(("gz", "dev")),
        ),
        out_specs=(columns, columns, columns),
        check_vma=False,
    )
```

```python
import functools

import jax
import jax.numpy as jnp
from jax import lax
from jax.experimental import pallas as pl
from jax.experimental.pallas import tpu as pltpu
from jax.sharding import PartitionSpec as P

MESH = pl.DeviceIdType.MESH
F32 = jnp.float32
BF16 = jnp.bfloat16
LANES = 128
ELEMENTS = 64
RIGHT = 8
NODES = 512
LOCAL = 384
ROWS = RIGHT * ELEMENTS
PAIRS = RIGHT // 2


def partner(me, turn, count):
    if count != 64:
        return (me + 1 + turn) % count
    far_z, far_y, far_core = turn // 8, turn % 8 // 2, turn % 2
    step_z = (4 + (far_z + 1) // 2 * (1 - 2 * (far_z % 2))) % 8
    step_y = (2 + (far_y + 1) // 2 * (1 - 2 * (far_y % 2))) % 4
    z = (me // 8 + step_z) % 8
    y = (me % 8 // 2 + step_y) % 4
    core = (me % 2 + 1 - far_core) % 2
    return z * 8 + y * 2 + core


def halves(value):
    high = value.astype(BF16)
    return high, (value - high.astype(F32)).astype(BF16)


def dot(left, right):
    return jnp.dot(left, right, preferred_element_type=F32)


def dot_three(left_high, left_low, right_high, right_low):
    return dot(left_high, right_high) + (dot(left_high, right_low) + dot(left_low, right_high))


def pick(onehot, value):
    high, low = halves(value)
    return dot(onehot, high) + dot(onehot, low)


def lane_of(shape):
    return lax.broadcasted_iota(jnp.int32, shape, 1)


def row_of(shape):
    return lax.broadcasted_iota(jnp.int32, shape, 0)


def swap_pair(first, second):
    low = lane_of(first.shape) < 64
    return (
        jnp.where(low, first, pltpu.roll(second, 64, 1)),
        jnp.where(low, pltpu.roll(first, 64, 1), second),
    )


def turned(value, index):
    return jnp.take_along_axis(value, index, axis=1, mode="promise_in_bounds")


def kernel(
    layers,
    blocks,
    source_hbm,
    inverse_hbm,
    coupling_hbm,
    operator_hbm,
    faces_hbm,
    codes_hbm,
    scale_hbm,
    solved,
    moved_zero,
    moved_one,
    sides_zero,
    sides_one,
    tops_zero,
    tops_one,
    weights,
    source,
    inverse,
    coupling,
    operator,
    faces_ref,
    codes_ref,
    scale_ref,
    source_h,
    source_l,
    inverse_h,
    inverse_l,
    coupling_h,
    coupling_l,
    operator_h,
    operator_l,
    merged_h,
    merged_l,
    merged_th,
    merged_tl,
    table,
    index_to,
    index_from,
    scales,
    first,
    image,
    update,
    vector_h,
    vector_l,
    slots_first,
    slots_second,
    bottoms,
    tops,
    second_image,
    sent,
    received,
    got_bottoms,
    got_tops,
    near_out,
    near_in,
    far_out,
    far_in,
    load_sem,
    swap_sem,
    up_sem,
    down_sem,
    near_sem,
    far_sem,
):
    layer = lax.axis_index("gz")
    me = lax.axis_index("dev")
    others = blocks - 1
    core = me % 2
    core_pair = me // 2 * 2

    barrier = pltpu.get_barrier_semaphore()

    def greet(turn, carry):
        pl.semaphore_signal(
            barrier, inc=1, device_id={"dev": partner(me, turn, blocks)}, device_id_type=MESH
        )
        return carry

    lax.fori_loop(0, others, greet, 0)
    for step in range(1, layers):
        for side in range(2):
            pl.semaphore_signal(
                barrier,
                inc=1,
                device_id=((layer + step) % layers, core_pair + (core + side) % 2),
                device_id_type=MESH,
            )

    loads = [
        pltpu.make_async_copy(inverse_hbm, inverse, load_sem.at[0]),
        pltpu.make_async_copy(coupling_hbm, coupling, load_sem.at[1]),
        pltpu.make_async_copy(source_hbm, source, load_sem.at[2]),
        pltpu.make_async_copy(operator_hbm, operator, load_sem.at[3]),
        pltpu.make_async_copy(faces_hbm, faces_ref, load_sem.at[4]),
        pltpu.make_async_copy(codes_hbm, codes_ref, load_sem.at[5]),
        pltpu.make_async_copy(scale_hbm, scale_ref, load_sem.at[6]),
    ]
    for load in loads[4:] + loads[:4]:
        load.start()

    here = pl.ds(pl.multiple_of(me * 8, 8), 8)
    for phase in range(3):
        received[phase, here, :] = jnp.zeros((8, LANES), F32)

    @pl.when(layer == 0)
    def _():
        got_bottoms[...] = jnp.zeros(got_bottoms.shape, F32)

    @pl.when(layer == layers - 1)
    def _():
        got_tops[...] = jnp.zeros(got_tops.shape, F32)

    table[...] = jnp.zeros(table.shape, F32)
    for load in loads[4:]:
        load.wait()
    faces = faces_ref[...].astype(F32)
    codes = codes_ref[...].astype(F32)
    for row in range(2):
        table[row : row + 1, 0:64] = faces[2 * row : 2 * row + 1]
        table[row : row + 1, 64:128] = faces[2 * row + 1 : 2 * row + 2]
    for row in range(3):
        table[2 + row : 3 + row, 0:64] = codes[2 * row : 2 * row + 1]
        table[2 + row : 3 + row, 64:128] = codes[2 * row + 1 : 2 * row + 2]
    table[5:6, 0:64] = scale_ref[...].astype(F32)
    columns = jnp.transpose(table[...])
    square = (LANES, LANES)
    first_row = jnp.broadcast_to(table[0:1, :], square).astype(jnp.int32) - me * LANES
    second_row = jnp.broadcast_to(table[1:2, :], square).astype(jnp.int32)
    first_col = jnp.broadcast_to(columns[:, 0:1], square).astype(jnp.int32) - me * LANES
    second_col = jnp.broadcast_to(columns[:, 1:2], square).astype(jnp.int32)

    def onehot(condition):
        return jnp.where(condition, 1.0, 0.0).astype(F32)

    near = onehot(first_col + me * LANES == second_row).astype(BF16)
    near_back = onehot(first_row + me * LANES == second_col).astype(BF16)
    into_faces = onehot(first_row == row_of(square)).astype(BF16)
    peers = (blocks, LANES)
    owner_row = second_row[:blocks] // LANES
    peer_row = row_of(peers)
    to_owner_f = onehot((owner_row == peer_row) & (peer_row != me))
    to_owner = to_owner_f.astype(BF16)
    from_owner = jnp.transpose(to_owner_f).astype(BF16)
    slot_number = (second_row[:blocks] % LANES + 1).astype(F32)
    named = jnp.sum(to_owner_f * slot_number, axis=1, keepdims=True)
    sent[0, pl.ds(4, blocks, stride=8), :] = jnp.broadcast_to(named, peers)

    lane = lane_of((ELEMENTS, LANES))
    low = lane < 64
    node_a, node_b = lane % 64 // 8, lane % 8
    for chunk in range(3):
        code = jnp.where(
            low,
            jnp.broadcast_to(columns[0:64, 2 + chunk : 3 + chunk], lane.shape),
            jnp.broadcast_to(columns[64:128, 2 + chunk : 3 + chunk], lane.shape),
        ).astype(jnp.int32)
        swapped, flip_a, flip_b = code // 4 % 2 == 1, code // 2 % 2 == 1, code % 2 == 1
        half = lane // 64 * 64
        a = jnp.where(flip_a, 7 - node_a, node_a)
        b = jnp.where(flip_b, 7 - node_b, node_b)
        index_to[chunk] = half + jnp.where(swapped, b * 8 + a, a * 8 + b)
        a = jnp.where(swapped, node_b, node_a)
        b = jnp.where(swapped, node_a, node_b)
        index_from[chunk] = half + jnp.where(flip_a, 7 - a, a) * 8 + jnp.where(flip_b, 7 - b, b)
    scales[...] = jnp.broadcast_to(columns[0:64, 5:6], scales.shape)
    live = (low & (layer > 0)) | ((lane >= 64) & (layer < layers - 1))

    def rows_of(right):
        return slice(right * ELEMENTS, (right + 1) * ELEMENTS)

    def lanes_of(chunk):
        return slice(chunk * LANES, (chunk + 1) * LANES)

    loads[0].wait()
    inverse_h[...], inverse_l[...] = halves(inverse[...])
    loads[1].wait()
    coupling_h[...], coupling_l[...] = halves(coupling[...])
    merged = dot_three(inverse_h[...], inverse_l[...], coupling_h[...], coupling_l[...])
    merged_h[...], merged_l[...] = halves(merged)
    loads[2].wait()
    source_h[...], source_l[...] = halves(source[...])
    image[...] = dot_three(source_h[...], source_l[...], merged_h[...], merged_l[...])

    def to_slots(vector, chunks, stores):
        for chunk in chunks:
            for pair in range(PAIRS):
                left = turned(vector[rows_of(2 * pair), lanes_of(chunk)], index_from[chunk])
                right = turned(vector[rows_of(2 * pair + 1), lanes_of(chunk)], index_from[chunk])
                stores[chunk](pair, *swap_pair(left, right))

    def store_slots(ref):
        def store(pair, even, odd):
            ref[0:64, lanes_of(pair)] = even
            ref[64:128, lanes_of(pair)] = odd

        return store

    def store_ends(pair, even, odd):
        bottoms[rows_of(pair), :] = even
        tops[rows_of(pair), :] = odd

    stores = (store_slots(slots_first), store_slots(slots_second), store_ends)

    def wait_rows(ref, rows, sem):
        whole = ref.at[pl.ds(0, rows)]
        pltpu.make_async_copy(whole, whole, sem).wait()

    def up_copy(phase):
        return pltpu.make_async_remote_copy(
            tops,
            got_bottoms.at[phase],
            up_sem.at[phase, 0],
            up_sem.at[phase, 1],
            device_id={"gz": layer + 1},
            device_id_type=MESH,
        )

    def down_copy(phase):
        return pltpu.make_async_remote_copy(
            bottoms,
            got_tops.at[phase],
            down_sem.at[phase, 0],
            down_sem.at[phase, 1],
            device_id={"gz": layer - 1},
            device_id_type=MESH,
        )

    def start_ends(phase):
        @pl.when(layer < layers - 1)
        def _():
            up_copy(phase).start()

        @pl.when(layer > 0)
        def _():
            down_copy(phase).start()

    def finish_ends(phase):
        @pl.when(layer < layers - 1)
        def _():
            up_copy(phase).wait_send()
            down_copy(phase).wait_recv()

        @pl.when(layer > 0)
        def _():
            down_copy(phase).wait_send()
            up_copy(phase).wait_recv()

    def send_rows(phase, rows):
        def send(turn, carry):
            peer = partner(me, turn, blocks)
            pltpu.make_async_remote_copy(
                sent.at[phase, pl.ds(pl.multiple_of(peer * 8, 8), rows)],
                received.at[phase, pl.ds(pl.multiple_of(me * 8, 8), rows)],
                swap_sem.at[phase, 0],
                swap_sem.at[phase, 1],
                device_id={"dev": peer},
                device_id_type=MESH,
            ).start()
            return carry

        lax.fori_loop(0, others, send, 0)

    def wait_sent(phase, rows):
        wait_rows(sent.at[phase], others * rows, swap_sem.at[phase, 0])

    def wait_received(phase, rows):
        wait_rows(received.at[phase], others * rows, swap_sem.at[phase, 1])

    def put(phase, first_row, value):
        for pair in range(PAIRS):
            sent[phase, pl.ds(first_row + pair, blocks, stride=8), :] = value[:, lanes_of(pair)]

    def got(phase, row):
        return received[phase, pl.ds(row, blocks, stride=8), :]

    def arrivals(chunk, pair, value):
        for offset, part in enumerate(swap_pair(value[0:64], value[64:128])):
            yield 2 * pair + offset, turned(part, index_to[chunk])

    def end_arrivals(phase):
        for pair in range(PAIRS):
            ends = got_bottoms[phase, rows_of(pair), :], got_tops[phase, rows_of(pair), :]
            for right, part in arrivals(2, pair, jnp.concatenate(ends, axis=0)):
                spot = rows_of(right), lanes_of(2)
                yield spot, jnp.where(live, image[spot] + part, 0.0)

    def keep(ref, spot, value):
        ref[spot] = value
        vector_h[spot], vector_l[spot] = halves(value)

    def sum_peer(turn):
        step = (layers // 2 + (turn // 2 + 1) // 2 * (1 - 2 * (turn // 2 % 2))) % layers
        return (layer + step) % layers, core_pair + (core + 1 - turn % 2) % 2

    def far_peer(turn):
        if blocks == 64:
            return partner(me, 2 * turn + 1, blocks)
        return (me + 2 * (turn + 1)) % blocks

    def start_sum(phase, quantities):
        lanes = lane_of((RIGHT, LANES))
        place = row_of((RIGHT, LANES))
        spread = jnp.zeros((RIGHT, LANES), F32)
        for number, rows in enumerate(quantities):
            total = jnp.sum(jnp.concatenate(rows, axis=0), axis=1, keepdims=True)
            spread = jnp.where(lanes == place + number * RIGHT, total, spread)
        mine = jnp.sum(spread, axis=0, keepdims=True)
        near_out[phase] = mine
        near_in[phase, layer * 2 + core] = mine

        def send(turn, carry):
            pltpu.make_async_remote_copy(
                near_out.at[phase],
                near_in.at[phase, layer * 2 + core],
                near_sem.at[phase, 0],
                near_sem.at[phase, 1],
                device_id=sum_peer(turn),
                device_id_type=MESH,
            ).start()
            return carry

        lax.fori_loop(0, 2 * layers - 1, send, 0)

    def middle_sum(phase):
        wait_rows(near_in.at[phase], 2 * layers - 1, near_sem.at[phase, 1])
        wait_rows(near_in.at[phase], 2 * layers - 1, near_sem.at[phase, 0])
        mine = jnp.sum(near_in[phase], axis=0)
        far_out[phase] = mine
        far_in[phase, me // 2] = mine

        def send(turn, carry):
            pltpu.make_async_remote_copy(
                far_out.at[phase],
                far_in.at[phase, me // 2],
                far_sem.at[phase, 0],
                far_sem.at[phase, 1],
                device_id={"dev": far_peer(turn)},
                device_id_type=MESH,
            ).start()
            return carry

        lax.fori_loop(0, blocks // 2 - 1, send, 0)

    def finish_sum(phase, count):
        wait_rows(far_in.at[phase], blocks // 2 - 1, far_sem.at[phase, 1])
        wait_rows(far_in.at[phase], blocks // 2 - 1, far_sem.at[phase, 0])
        total = jnp.broadcast_to(jnp.sum(far_in[phase], axis=0), (RIGHT, LANES))
        lanes = lane_of((RIGHT, LANES))
        place = row_of((RIGHT, LANES))
        return [
            jnp.broadcast_to(
                jnp.sum(
                    jnp.where(lanes == place + number * RIGHT, total, 0.0), axis=1, keepdims=True
                ),
                (RIGHT, LANES),
            )
            for number in range(count)
        ]

    def owned_square(values):
        kept = values[0] * values[0] + jnp.where(low, 0.0, values[2] * values[2])
        return jnp.sum(kept, axis=0, keepdims=True)

    def inner_rows(left, right):
        kept = left[0] * right[0] + left[1] * right[1] + left[2] * right[2]
        return jnp.sum(kept, axis=0, keepdims=True)

    def chunks_of(ref, right):
        return [ref[rows_of(right), lanes_of(chunk)] for chunk in range(3)]

    def operated(chunks):
        return sum(
            dot_three(
                vector_h[:, lanes_of(chunk)],
                vector_l[:, lanes_of(chunk)],
                operator_h[lanes_of(chunk), :],
                operator_l[lanes_of(chunk), :],
            )
            for chunk in chunks
        )

    def face_values(vector, sides_ref, tops_ref):
        for pair in range(PAIRS):
            for chunk in (0, 2):
                left = turned(vector[rows_of(2 * pair), lanes_of(chunk)], index_from[chunk])
                right = turned(vector[rows_of(2 * pair + 1), lanes_of(chunk)], index_from[chunk])
                even, odd = swap_pair(left, right)
                if chunk == 0:
                    turned_back = jnp.transpose(
                        pick(into_faces, jnp.concatenate([even, odd], axis=0))
                    )
                    target = sides_ref
                else:
                    turned_back = jnp.transpose(odd)
                    target = tops_ref
                for offset in range(2):
                    target[pl.ds(2 * pair + offset, 64, stride=8), :] = turned_back[
                        offset * 64 : (offset + 1) * 64
                    ]

    to_slots(image, (2, 1, 0), stores)
    put(0, 0, pick(to_owner, slots_second[...]))
    pl.semaphore_wait(barrier, others + 2 * (layers - 1))

    send_rows(0, 5)
    start_ends(0)
    solved[...] = dot_three(source_h[...], source_l[...], inverse_h[...], inverse_l[...])
    loads[3].wait()
    operator_h[...], operator_l[...] = halves(operator[...])
    nearby_first = pick(near, slots_second[...])
    wait_received(0, 5)
    to_holder_f = onehot(got(0, 4).astype(jnp.int32) == first_row[:blocks] + 1)
    to_holder = to_holder_f.astype(BF16)
    from_holder = jnp.transpose(to_holder_f).astype(BF16)

    put(1, 0, pick(to_holder, slots_first[...]))
    send_rows(1, 4)
    for pair in range(PAIRS):
        value = nearby_first[:, lanes_of(pair)] + pick(from_holder, got(0, pair))
        for right, part in arrivals(0, pair, value):
            spot = rows_of(right), lanes_of(0)
            keep(first, spot, image[spot] + part)
    finish_ends(0)
    for spot, value in end_arrivals(0):
        keep(first, spot, value)
    second_image[...] = operated((0, 2))
    nearby_second = pick(near_back, slots_first[...])
    wait_received(1, 4)
    for pair in range(PAIRS):
        value = nearby_second[:, lanes_of(pair)] + pick(from_owner, got(1, pair))
        for right, part in arrivals(1, pair, value):
            spot = rows_of(right), lanes_of(1)
            keep(first, spot, image[spot] + part)
    image[...] = second_image[...] + operated((1,))

    squares, curves = [], []
    for right in range(RIGHT):
        for chunk in range(3):
            image[rows_of(right), lanes_of(chunk)] = image[rows_of(right), lanes_of(chunk)] * scales[...]
        mine = chunks_of(first, right)
        squares.append(owned_square(mine))
        curves.append(inner_rows(mine, chunks_of(image, right)))
    start_sum(0, [squares, curves])
    wait_sent(0, 5)
    wait_sent(1, 4)
    to_slots(image, (1, 0, 2), stores)
    put(2, 0, pick(to_owner, slots_second[...]))
    put(2, 4, pick(to_holder, slots_first[...]))
    send_rows(2, 8)
    start_ends(1)

    middle_sum(0)
    nearby_first = pick(near, slots_second[...])
    nearby_second = pick(near_back, slots_first[...])
    for right in range(RIGHT):
        for part in range(4):
            solved[rows_of(right), lanes_of(part)] = solved[rows_of(right), lanes_of(part)] / scales[...]
    merged_th[...] = jnp.transpose(merged_h[...].astype(F32)).astype(BF16)
    merged_tl[...] = jnp.transpose(merged_l[...].astype(F32)).astype(BF16)
    moved_zero[...] = dot_three(vector_h[...], vector_l[...], merged_th[...], merged_tl[...])
    face_values(first, sides_zero, tops_zero)
    finish_ends(1)
    for spot, value in end_arrivals(1):
        keep(update, spot, value)
    wait_received(2, 8)
    wait_sent(2, 8)
    for pair in range(PAIRS):
        arrived = (
            nearby_first[:, lanes_of(pair)] + pick(from_holder, got(2, pair)),
            nearby_second[:, lanes_of(pair)] + pick(from_owner, got(2, pair + 4)),
        )
        for chunk in range(2):
            for right, part in arrivals(chunk, pair, arrived[chunk]):
                spot = rows_of(right), lanes_of(chunk)
                keep(update, spot, image[spot] + part)
    second_image[...] = operated((0, 1, 2))

    norm, curve = finish_sum(0, 2)
    alpha = norm / curve
    squares, crosses, curves = [], [], []
    for right in range(RIGHT):
        step = alpha[right : right + 1, :]
        before, change = chunks_of(first, right), chunks_of(update, right)
        old, turned_change = chunks_of(image, right), chunks_of(second_image, right)
        mine = [before[chunk] - step * change[chunk] for chunk in range(3)]
        new = [old[chunk] - step * (turned_change[chunk] * scales[...]) for chunk in range(3)]
        squares.append(owned_square(mine))
        crosses.append(inner_rows(mine, old))
        curves.append(inner_rows(mine, new))
    start_sum(1, [squares, crosses, curves])

    moved_one[...] = dot_three(vector_h[...], vector_l[...], merged_th[...], merged_tl[...])
    middle_sum(1)
    face_values(update, sides_one, tops_one)
    norm_next, cross, curve_next = finish_sum(1, 3)
    beta = norm_next / norm
    curve_next = curve_next + 2.0 * beta * cross + beta * beta * curve
    weight_update = norm_next / curve_next
    weights[0:8, :] = alpha + weight_update * beta + weight_update
    weights[8:16, :] = weight_update * alpha


def combine(weights, solved, moved_zero, moved_one, sides_zero, sides_one, tops_zero, tops_one, interior, sides, tops):
    for right in range(RIGHT):
        for part in range(4):
            spot = slice(right * 64, right * 64 + 64), slice(part * LANES, part * LANES + LANES)
            interior[spot] = (
                solved[spot]
                - weights[right : right + 1, :] * moved_zero[spot]
                + weights[8 + right : 9 + right, :] * moved_one[spot]
            )
    for node in range(64):
        spot = slice(node * 8, node * 8 + 8)
        sides[spot, :] = weights[0:8, :] * sides_zero[spot, :] - weights[8:16, :] * sides_one[spot, :]
        tops[spot, :] = weights[0:8, :64] * tops_zero[spot, :] - weights[8:16, :64] * tops_one[spot, :]


def solution(mesh):
    layers, blocks = mesh.shape["gz"], mesh.shape["dev"]

    def per_device(source, inverse, coupling, operator, face_ids, orientation, scale):
        flat = source.transpose(1, 2, 0).reshape(ROWS, NODES)
        vmem = pltpu.VMEM
        far = pl.BlockSpec(memory_space=pltpu.HBM)
        local = pl.BlockSpec(memory_space=pltpu.VMEM)
        dma = pltpu.SemaphoreType.DMA
        shapes = [
            *[jax.ShapeDtypeStruct((ROWS, NODES), F32)] * 3,
            *[jax.ShapeDtypeStruct((512, 128), F32)] * 2,
            *[jax.ShapeDtypeStruct((512, 64), F32)] * 2,
            jax.ShapeDtypeStruct((16, LANES), F32),
        ]
        *found, weights = pl.pallas_call(
            functools.partial(kernel, layers, blocks),
            out_shape=tuple(shapes),
            in_specs=[far] * 7,
            out_specs=(local,) * 8,
            scratch_shapes=[
                vmem((ROWS, NODES), F32),
                vmem((NODES, NODES), F32),
                vmem((NODES, LOCAL), F32),
                vmem((LOCAL, LOCAL), F32),
                vmem((4, ELEMENTS), jnp.int32),
                vmem((6, ELEMENTS), jnp.int32),
                vmem((1, ELEMENTS), jnp.int32),
                *[vmem((ROWS, NODES), BF16)] * 2,
                *[vmem((NODES, NODES), BF16)] * 2,
                *[vmem((NODES, LOCAL), BF16)] * 2,
                *[vmem((LOCAL, LOCAL), BF16)] * 2,
                *[vmem((NODES, LOCAL), BF16)] * 2,
                *[vmem((LOCAL, NODES), BF16)] * 2,
                vmem((LANES, LANES), F32),
                vmem((3, ELEMENTS, LANES), jnp.int32),
                vmem((3, ELEMENTS, LANES), jnp.int32),
                vmem((ELEMENTS, LANES), F32),
                *[vmem((ROWS, LOCAL), F32)] * 3,
                *[vmem((ROWS, LOCAL), BF16)] * 2,
                *[vmem((128, 512), F32)] * 2,
                *[vmem((256, 128), F32)] * 2,
                vmem((ROWS, LOCAL), F32),
                *[vmem((3, blocks * 8, LANES), F32)] * 2,
                *[vmem((2, 256, 128), F32)] * 2,
                vmem((2, 1, LANES), F32),
                vmem((2, 2 * layers, 1, LANES), F32),
                vmem((2, 1, LANES), F32),
                vmem((2, blocks // 2, 1, LANES), F32),
                dma((7,)),
                dma((3, 2)),
                dma((2, 2)),
                dma((2, 2)),
                dma((2, 2)),
                dma((2, 2)),
            ],
            compiler_params=pltpu.CompilerParams(
                collective_id=0, has_side_effects=True, vmem_limit_bytes=32 << 20
            ),
        )(
            *(
                pltpu.with_memory_space_constraint(value, pltpu.HBM)
                for value in (
                    flat,
                    inverse,
                    coupling,
                    operator,
                    face_ids.T,
                    orientation.T,
                    scale.reshape(1, ELEMENTS),
                )
            )
        )
        interior, sides, tops = pl.pallas_call(
            combine,
            out_shape=(shapes[0], shapes[3], shapes[5]),
            in_specs=[local] * 8,
            out_specs=(local,) * 3,
            compiler_params=pltpu.CompilerParams(vmem_limit_bytes=16 << 20),
        )(weights, *found)
        return (
            interior.reshape(RIGHT, ELEMENTS, NODES).transpose(2, 0, 1),
            sides.reshape(64, RIGHT, 128),
            tops.reshape(64, RIGHT, ELEMENTS),
        )

    columns = P(None, None, ("gz", "dev"))
    return jax.shard_map(
        per_device,
        mesh=mesh,
        in_specs=(
            columns,
            P(),
            P(),
            P(),
            P(("gz", "dev"), None),
            P(("gz", "dev"), None),
            P(("gz", "dev")),
        ),
        out_specs=(columns, columns, columns),
        check_vma=False,
    )
```

```python
import functools

import jax
import jax.numpy as jnp
from jax import lax
from jax.experimental import pallas as pl
from jax.experimental.pallas import tpu as pltpu
from jax.sharding import PartitionSpec as P

MESH = pl.DeviceIdType.MESH
F32 = jnp.float32
BF16 = jnp.bfloat16
LANES = 128
ELEMENTS = 64
RIGHT = 8
NODES = 512
LOCAL = 384
ROWS = RIGHT * ELEMENTS
PAIRS = RIGHT // 2


def turns(layers, blocks):
    def ring(step, count):
        return min(step, count - step)

    deep = blocks // 8
    steps = [
        (x, z, y, core)
        for x in range(layers)
        for z in range(deep)
        for y in range(4)
        for core in (1, 0)
        if (x, z, y, core) != (0, 0, 0, 0)
    ]
    return sorted(
        steps, key=lambda step: (-ring(step[0], layers) - ring(step[1], deep) - ring(step[2], 4), step[3])
    )


def halves(value):
    high = value.astype(BF16)
    return high, (value - high.astype(F32)).astype(BF16)


def dot(left, right):
    return jnp.dot(left, right, preferred_element_type=F32)


def dot_three(left_high, left_low, right_high, right_low):
    return dot(left_high, right_high) + (dot(left_high, right_low) + dot(left_low, right_high))


def pick(onehot, value):
    high, low = halves(value)
    return dot(onehot, high) + dot(onehot, low)


def lane_of(shape):
    return lax.broadcasted_iota(jnp.int32, shape, 1)


def row_of(shape):
    return lax.broadcasted_iota(jnp.int32, shape, 0)


def swap_pair(first, second):
    low = lane_of(first.shape) < 64
    return (
        jnp.where(low, first, pltpu.roll(second, 64, 1)),
        jnp.where(low, pltpu.roll(first, 64, 1), second),
    )


def turned(value, index):
    return jnp.take_along_axis(value, index, axis=1, mode="promise_in_bounds")


def kernel(
    layers,
    blocks,
    source_hbm,
    inverse_hbm,
    coupling_hbm,
    operator_hbm,
    faces_hbm,
    codes_hbm,
    scale_hbm,
    solved,
    moved_zero,
    moved_one,
    sides_zero,
    sides_one,
    tops_zero,
    tops_one,
    weights,
    source,
    inverse,
    coupling,
    operator,
    faces_ref,
    codes_ref,
    scale_ref,
    source_h,
    source_l,
    inverse_h,
    inverse_l,
    coupling_h,
    coupling_l,
    operator_h,
    operator_l,
    merged_h,
    merged_l,
    merged_th,
    merged_tl,
    table,
    index_to,
    index_from,
    scales,
    first,
    image,
    update,
    vector_h,
    vector_l,
    slots_first,
    slots_second,
    bottoms,
    tops,
    second_image,
    sent,
    received,
    got_bottoms,
    got_tops,
    near_out,
    near_in,
    far_out,
    far_in,
    load_sem,
    swap_sem,
    up_sem,
    down_sem,
    near_sem,
    far_sem,
):
    layer = lax.axis_index("gz")
    me = lax.axis_index("dev")
    others = blocks - 1
    core = me % 2

    deep = blocks // 8
    along_x = [(layer + step) % layers for step in range(layers)]
    along_z = [(me // 8 + step) % deep * 8 for step in range(deep)]
    along_y = [(me % 8 // 2 + step) % 4 * 2 for step in range(4)]
    along_core = [core, 1 - core]
    everyone = [
        (x, z, y, c, along_x[x], along_z[z] + along_y[y] + along_core[c])
        for x, z, y, c in turns(layers, blocks)
    ]
    peers = [peer for x, *_, peer in everyone if x == 0]
    column_peers = [(at, peer) for x, z, y, _, at, peer in everyone if z == 0 and y == 0]
    far_peers = [peer for x, _, _, c, _, peer in everyone if x == 0 and c == 0]

    barrier = pltpu.get_barrier_semaphore()
    for peer in peers:
        pl.semaphore_signal(barrier, inc=1, device_id=(layer, peer), device_id_type=MESH)
    for at, peer in column_peers:
        if at is not along_x[0]:
            pl.semaphore_signal(barrier, inc=1, device_id=(at, peer), device_id_type=MESH)

    loads = [
        pltpu.make_async_copy(inverse_hbm, inverse, load_sem.at[0]),
        pltpu.make_async_copy(coupling_hbm, coupling, load_sem.at[1]),
        pltpu.make_async_copy(source_hbm, source, load_sem.at[2]),
        pltpu.make_async_copy(operator_hbm, operator, load_sem.at[3]),
        pltpu.make_async_copy(faces_hbm, faces_ref, load_sem.at[4]),
        pltpu.make_async_copy(codes_hbm, codes_ref, load_sem.at[5]),
        pltpu.make_async_copy(scale_hbm, scale_ref, load_sem.at[6]),
    ]
    for load in loads[4:] + loads[:4]:
        load.start()

    here = pl.ds(pl.multiple_of(me * 8, 8), 8)
    for phase in range(4):
        received[phase, here, :] = jnp.zeros((8, LANES), F32)

    @pl.when(layer == 0)
    def _():
        got_bottoms[...] = jnp.zeros(got_bottoms.shape, F32)

    @pl.when(layer == layers - 1)
    def _():
        got_tops[...] = jnp.zeros(got_tops.shape, F32)

    table[...] = jnp.zeros(table.shape, F32)
    for load in loads[4:]:
        load.wait()
    faces = faces_ref[...].astype(F32)
    codes = codes_ref[...].astype(F32)
    for row in range(2):
        table[row : row + 1, 0:64] = faces[2 * row : 2 * row + 1]
        table[row : row + 1, 64:128] = faces[2 * row + 1 : 2 * row + 2]
    for row in range(3):
        table[2 + row : 3 + row, 0:64] = codes[2 * row : 2 * row + 1]
        table[2 + row : 3 + row, 64:128] = codes[2 * row + 1 : 2 * row + 2]
    table[5:6, 0:64] = scale_ref[...].astype(F32)
    columns = jnp.transpose(table[...])
    square = (LANES, LANES)
    first_row = jnp.broadcast_to(table[0:1, :], square).astype(jnp.int32) - me * LANES
    second_row = jnp.broadcast_to(table[1:2, :], square).astype(jnp.int32)
    first_col = jnp.broadcast_to(columns[:, 0:1], square).astype(jnp.int32) - me * LANES
    second_col = jnp.broadcast_to(columns[:, 1:2], square).astype(jnp.int32)

    def onehot(condition):
        return jnp.where(condition, 1.0, 0.0).astype(F32)

    near = onehot(first_col + me * LANES == second_row).astype(BF16)
    near_back = onehot(first_row + me * LANES == second_col).astype(BF16)
    into_faces = onehot(first_row == row_of(square)).astype(BF16)
    peer_shape = (blocks, LANES)
    owner_row = second_row[:blocks] // LANES
    peer_row = row_of(peer_shape)
    to_owner_f = onehot((owner_row == peer_row) & (peer_row != me))
    to_owner = to_owner_f.astype(BF16)
    from_owner = jnp.transpose(to_owner_f).astype(BF16)
    slot_number = (second_row[:blocks] % LANES + 1).astype(F32)
    named = jnp.sum(to_owner_f * slot_number, axis=1, keepdims=True)
    sent[3, pl.ds(0, blocks, stride=8), :] = jnp.broadcast_to(named, peer_shape)

    lane = lane_of((ELEMENTS, LANES))
    low = lane < 64
    node_a, node_b = lane % 64 // 8, lane % 8
    for chunk in range(3):
        code = jnp.where(
            low,
            jnp.broadcast_to(columns[0:64, 2 + chunk : 3 + chunk], lane.shape),
            jnp.broadcast_to(columns[64:128, 2 + chunk : 3 + chunk], lane.shape),
        ).astype(jnp.int32)
        swapped, flip_a, flip_b = code // 4 % 2 == 1, code // 2 % 2 == 1, code % 2 == 1
        half = lane // 64 * 64
        a = jnp.where(flip_a, 7 - node_a, node_a)
        b = jnp.where(flip_b, 7 - node_b, node_b)
        index_to[chunk] = half + jnp.where(swapped, b * 8 + a, a * 8 + b)
        a = jnp.where(swapped, node_b, node_a)
        b = jnp.where(swapped, node_a, node_b)
        index_from[chunk] = half + jnp.where(flip_a, 7 - a, a) * 8 + jnp.where(flip_b, 7 - b, b)
    scales[...] = jnp.broadcast_to(columns[0:64, 5:6], scales.shape)
    live = (low & (layer > 0)) | ((lane >= 64) & (layer < layers - 1))

    def rows_of(right):
        return slice(right * ELEMENTS, (right + 1) * ELEMENTS)

    def lanes_of(chunk):
        return slice(chunk * LANES, (chunk + 1) * LANES)

    loads[0].wait()
    inverse_h[...], inverse_l[...] = halves(inverse[...])
    loads[1].wait()
    coupling_h[...], coupling_l[...] = halves(coupling[...])
    merged = dot_three(inverse_h[...], inverse_l[...], coupling_h[...], coupling_l[...])
    merged_h[...], merged_l[...] = halves(merged)
    loads[2].wait()
    source_h[...], source_l[...] = halves(source[...])
    image[...] = dot_three(source_h[...], source_l[...], merged_h[...], merged_l[...])

    def to_slots(vector, chunks, stores):
        for chunk in chunks:
            for pair in range(PAIRS):
                left = turned(vector[rows_of(2 * pair), lanes_of(chunk)], index_from[chunk])
                right = turned(vector[rows_of(2 * pair + 1), lanes_of(chunk)], index_from[chunk])
                stores[chunk](pair, *swap_pair(left, right))

    def store_slots(ref):
        def store(pair, even, odd):
            ref[0:64, lanes_of(pair)] = even
            ref[64:128, lanes_of(pair)] = odd

        return store

    def store_ends(pair, even, odd):
        bottoms[rows_of(pair), :] = even
        tops[rows_of(pair), :] = odd

    stores = (store_slots(slots_first), store_slots(slots_second), store_ends)

    def wait_rows(ref, rows, sem):
        whole = ref.at[pl.ds(0, rows)]
        pltpu.make_async_copy(whole, whole, sem).wait()

    def up_copy(phase):
        return pltpu.make_async_remote_copy(
            tops,
            got_bottoms.at[phase],
            up_sem.at[phase, 0],
            up_sem.at[phase, 1],
            device_id={"gz": layer + 1},
            device_id_type=MESH,
        )

    def down_copy(phase):
        return pltpu.make_async_remote_copy(
            bottoms,
            got_tops.at[phase],
            down_sem.at[phase, 0],
            down_sem.at[phase, 1],
            device_id={"gz": layer - 1},
            device_id_type=MESH,
        )

    def start_ends(phase):
        @pl.when(layer < layers - 1)
        def _():
            up_copy(phase).start()

        @pl.when(layer > 0)
        def _():
            down_copy(phase).start()

    def finish_ends(phase):
        @pl.when(layer < layers - 1)
        def _():
            up_copy(phase).wait_send()
            down_copy(phase).wait_recv()

        @pl.when(layer > 0)
        def _():
            down_copy(phase).wait_send()
            up_copy(phase).wait_recv()

    def send_rows(phase, rows):
        for peer in peers:
            pltpu.make_async_remote_copy(
                sent.at[phase, pl.ds(pl.multiple_of(peer * 8, 8), rows)],
                received.at[phase, pl.ds(pl.multiple_of(me * 8, 8), rows)],
                swap_sem.at[phase, 0],
                swap_sem.at[phase, 1],
                device_id=(layer, peer),
                device_id_type=MESH,
            ).start()

    def wait_sent(phase, rows):
        wait_rows(sent.at[phase], others * rows, swap_sem.at[phase, 0])

    def wait_received(phase, rows):
        wait_rows(received.at[phase], others * rows, swap_sem.at[phase, 1])

    def put(phase, first_row, value):
        for pair in range(PAIRS):
            sent[phase, pl.ds(first_row + pair, blocks, stride=8), :] = value[:, lanes_of(pair)]

    def got(phase, row):
        return received[phase, pl.ds(row, blocks, stride=8), :]

    def arrivals(chunk, pair, value):
        for offset, part in enumerate(swap_pair(value[0:64], value[64:128])):
            yield 2 * pair + offset, turned(part, index_to[chunk])

    def end_arrivals(phase):
        for pair in range(PAIRS):
            ends = got_bottoms[phase, rows_of(pair), :], got_tops[phase, rows_of(pair), :]
            for right, part in arrivals(2, pair, jnp.concatenate(ends, axis=0)):
                spot = rows_of(right), lanes_of(2)
                yield spot, jnp.where(live, image[spot] + part, 0.0)

    def keep(ref, spot, value):
        ref[spot] = value
        vector_h[spot], vector_l[spot] = halves(value)

    def summed(quantities):
        lanes = lane_of((RIGHT, LANES))
        place = row_of((RIGHT, LANES))
        spread = jnp.zeros((RIGHT, LANES), F32)
        for number, rows in enumerate(quantities):
            total = jnp.sum(jnp.concatenate(rows, axis=0), axis=1, keepdims=True)
            spread = jnp.where(lanes == place + number * RIGHT, total, spread)
        return jnp.sum(spread, axis=0, keepdims=True)

    def share(mine, out_ref, in_ref, place, sem, targets):
        out_ref[...] = mine
        in_ref[place] = mine
        for at, peer in targets:
            pltpu.make_async_remote_copy(
                out_ref,
                in_ref.at[place],
                sem.at[0],
                sem.at[1],
                device_id=(at, peer),
                device_id_type=MESH,
            ).start()

    def shared(in_ref, sem, count):
        wait_rows(in_ref, count, sem.at[1])
        wait_rows(in_ref, count, sem.at[0])
        return jnp.sum(in_ref[...], axis=0)

    def share_near(phase, quantities):
        share(
            summed(quantities),
            near_out.at[phase],
            near_in.at[phase],
            layer * 2 + core,
            near_sem.at[phase],
            column_peers,
        )

    def share_far(phase):
        share(
            shared(near_in.at[phase], near_sem.at[phase], len(column_peers)),
            far_out.at[phase],
            far_in.at[phase],
            me // 2,
            far_sem.at[phase],
            [(layer, peer) for peer in far_peers],
        )

    def columns_of(row, count):
        total = jnp.broadcast_to(row, (RIGHT, LANES))
        lanes = lane_of((RIGHT, LANES))
        place = row_of((RIGHT, LANES))
        return [
            jnp.broadcast_to(
                jnp.sum(
                    jnp.where(lanes == place + number * RIGHT, total, 0.0), axis=1, keepdims=True
                ),
                (RIGHT, LANES),
            )
            for number in range(count)
        ]

    def finish_far(phase, count):
        return columns_of(shared(far_in.at[phase], far_sem.at[phase], len(far_peers)), count)

    def owned_square(values):
        kept = values[0] * values[0] + jnp.where(low, 0.0, values[2] * values[2])
        return jnp.sum(kept, axis=0, keepdims=True)

    def inner_rows(left, right):
        kept = left[0] * right[0] + left[1] * right[1] + left[2] * right[2]
        return jnp.sum(kept, axis=0, keepdims=True)

    def chunks_of(ref, right):
        return [ref[rows_of(right), lanes_of(chunk)] for chunk in range(3)]

    def operated(chunks):
        return sum(
            dot_three(
                vector_h[:, lanes_of(chunk)],
                vector_l[:, lanes_of(chunk)],
                operator_h[lanes_of(chunk), :],
                operator_l[lanes_of(chunk), :],
            )
            for chunk in chunks
        )

    def face_values(vector, sides_ref, tops_ref):
        for pair in range(PAIRS):
            for chunk in (0, 2):
                left = turned(vector[rows_of(2 * pair), lanes_of(chunk)], index_from[chunk])
                right = turned(vector[rows_of(2 * pair + 1), lanes_of(chunk)], index_from[chunk])
                even, odd = swap_pair(left, right)
                if chunk == 0:
                    turned_back = jnp.transpose(
                        pick(into_faces, jnp.concatenate([even, odd], axis=0))
                    )
                    target = sides_ref
                else:
                    turned_back = jnp.transpose(odd)
                    target = tops_ref
                for offset in range(2):
                    target[pl.ds(2 * pair + offset, 64, stride=8), :] = turned_back[
                        offset * 64 : (offset + 1) * 64
                    ]

    to_slots(image, (2, 1, 0), stores)
    put(0, 0, pick(to_owner, slots_second[...]))
    pl.semaphore_wait(barrier, others + 2 * (layers - 1))

    send_rows(3, 1)
    send_rows(0, 4)
    start_ends(0)
    solved[...] = dot_three(source_h[...], source_l[...], inverse_h[...], inverse_l[...])
    loads[3].wait()
    operator_h[...], operator_l[...] = halves(operator[...])
    nearby_first = pick(near, slots_second[...])
    wait_received(3, 1)
    to_holder_f = onehot(got(3, 0).astype(jnp.int32) == first_row[:blocks] + 1)
    to_holder = to_holder_f.astype(BF16)
    from_holder = jnp.transpose(to_holder_f).astype(BF16)

    put(1, 0, pick(to_holder, slots_first[...]))
    send_rows(1, 4)
    wait_received(0, 4)
    for pair in range(PAIRS):
        value = nearby_first[:, lanes_of(pair)] + pick(from_holder, got(0, pair))
        for right, part in arrivals(0, pair, value):
            spot = rows_of(right), lanes_of(0)
            keep(first, spot, image[spot] + part)
    finish_ends(0)
    for spot, value in end_arrivals(0):
        keep(first, spot, value)
    second_image[...] = operated((0, 2))
    nearby_second = pick(near_back, slots_first[...])
    wait_received(1, 4)
    for pair in range(PAIRS):
        value = nearby_second[:, lanes_of(pair)] + pick(from_owner, got(1, pair))
        for right, part in arrivals(1, pair, value):
            spot = rows_of(right), lanes_of(1)
            keep(first, spot, image[spot] + part)
    image[...] = second_image[...] + operated((1,))

    squares, curves = [], []
    for right in range(RIGHT):
        for chunk in range(3):
            image[rows_of(right), lanes_of(chunk)] = image[rows_of(right), lanes_of(chunk)] * scales[...]
        mine = chunks_of(first, right)
        squares.append(owned_square(mine))
        curves.append(inner_rows(mine, chunks_of(image, right)))
    share_near(0, [squares, curves])
    wait_sent(3, 1)
    wait_sent(0, 4)
    wait_sent(1, 4)
    to_slots(image, (1, 0, 2), stores)
    put(2, 0, pick(to_owner, slots_second[...]))
    put(2, 4, pick(to_holder, slots_first[...]))
    send_rows(2, 8)
    start_ends(1)

    share_far(0)
    nearby_first = pick(near, slots_second[...])
    nearby_second = pick(near_back, slots_first[...])
    for right in range(RIGHT):
        for part in range(4):
            solved[rows_of(right), lanes_of(part)] = solved[rows_of(right), lanes_of(part)] / scales[...]
    merged_th[...] = jnp.transpose(merged_h[...].astype(F32)).astype(BF16)
    merged_tl[...] = jnp.transpose(merged_l[...].astype(F32)).astype(BF16)
    moved_zero[...] = dot_three(vector_h[...], vector_l[...], merged_th[...], merged_tl[...])
    face_values(first, sides_zero, tops_zero)
    finish_ends(1)
    for spot, value in end_arrivals(1):
        keep(update, spot, value)
    wait_received(2, 8)
    wait_sent(2, 8)
    for pair in range(PAIRS):
        arrived = (
            nearby_first[:, lanes_of(pair)] + pick(from_holder, got(2, pair)),
            nearby_second[:, lanes_of(pair)] + pick(from_owner, got(2, pair + 4)),
        )
        for chunk in range(2):
            for right, part in arrivals(chunk, pair, arrived[chunk]):
                spot = rows_of(right), lanes_of(chunk)
                keep(update, spot, image[spot] + part)
    second_image[...] = operated((0, 1, 2))

    norm, curve = finish_far(0, 2)
    alpha = norm / curve
    squares, crosses, curves = [], [], []
    for right in range(RIGHT):
        step = alpha[right : right + 1, :]
        before, change = chunks_of(first, right), chunks_of(update, right)
        old, turned_change = chunks_of(image, right), chunks_of(second_image, right)
        mine = [before[chunk] - step * change[chunk] for chunk in range(3)]
        new = [old[chunk] - step * (turned_change[chunk] * scales[...]) for chunk in range(3)]
        squares.append(owned_square(mine))
        crosses.append(inner_rows(mine, old))
        curves.append(inner_rows(mine, new))
    share_near(1, [squares, crosses, curves])

    moved_one[...] = dot_three(vector_h[...], vector_l[...], merged_th[...], merged_tl[...])
    share_far(1)
    face_values(update, sides_one, tops_one)
    norm_next, cross, curve_next = finish_far(1, 3)
    beta = norm_next / norm
    curve_next = curve_next + 2.0 * beta * cross + beta * beta * curve
    weight_update = norm_next / curve_next
    weights[0:8, :] = alpha + weight_update * beta + weight_update
    weights[8:16, :] = weight_update * alpha


def combine(weights, solved, moved_zero, moved_one, sides_zero, sides_one, tops_zero, tops_one, interior, sides, tops):
    for right in range(RIGHT):
        for part in range(4):
            spot = slice(right * 64, right * 64 + 64), slice(part * LANES, part * LANES + LANES)
            interior[spot] = (
                solved[spot]
                - weights[right : right + 1, :] * moved_zero[spot]
                + weights[8 + right : 9 + right, :] * moved_one[spot]
            )
    for node in range(64):
        spot = slice(node * 8, node * 8 + 8)
        sides[spot, :] = weights[0:8, :] * sides_zero[spot, :] - weights[8:16, :] * sides_one[spot, :]
        tops[spot, :] = weights[0:8, :64] * tops_zero[spot, :] - weights[8:16, :64] * tops_one[spot, :]


def solution(mesh):
    layers, blocks = mesh.shape["gz"], mesh.shape["dev"]

    def per_device(source, inverse, coupling, operator, face_ids, orientation, scale):
        flat = source.transpose(1, 2, 0).reshape(ROWS, NODES)
        vmem = pltpu.VMEM
        far = pl.BlockSpec(memory_space=pltpu.HBM)
        local = pl.BlockSpec(memory_space=pltpu.VMEM)
        dma = pltpu.SemaphoreType.DMA
        shapes = [
            *[jax.ShapeDtypeStruct((ROWS, NODES), F32)] * 3,
            *[jax.ShapeDtypeStruct((512, 128), F32)] * 2,
            *[jax.ShapeDtypeStruct((512, 64), F32)] * 2,
            jax.ShapeDtypeStruct((16, LANES), F32),
        ]
        *found, weights = pl.pallas_call(
            functools.partial(kernel, layers, blocks),
            out_shape=tuple(shapes),
            in_specs=[far] * 7,
            out_specs=(local,) * 8,
            scratch_shapes=[
                vmem((ROWS, NODES), F32),
                vmem((NODES, NODES), F32),
                vmem((NODES, LOCAL), F32),
                vmem((LOCAL, LOCAL), F32),
                vmem((4, ELEMENTS), jnp.int32),
                vmem((6, ELEMENTS), jnp.int32),
                vmem((1, ELEMENTS), jnp.int32),
                *[vmem((ROWS, NODES), BF16)] * 2,
                *[vmem((NODES, NODES), BF16)] * 2,
                *[vmem((NODES, LOCAL), BF16)] * 2,
                *[vmem((LOCAL, LOCAL), BF16)] * 2,
                *[vmem((NODES, LOCAL), BF16)] * 2,
                *[vmem((LOCAL, NODES), BF16)] * 2,
                vmem((LANES, LANES), F32),
                vmem((3, ELEMENTS, LANES), jnp.int32),
                vmem((3, ELEMENTS, LANES), jnp.int32),
                vmem((ELEMENTS, LANES), F32),
                *[vmem((ROWS, LOCAL), F32)] * 3,
                *[vmem((ROWS, LOCAL), BF16)] * 2,
                *[vmem((128, 512), F32)] * 2,
                *[vmem((256, 128), F32)] * 2,
                vmem((ROWS, LOCAL), F32),
                *[vmem((4, blocks * 8, LANES), F32)] * 2,
                *[vmem((2, 256, 128), F32)] * 2,
                vmem((2, 1, LANES), F32),
                vmem((2, 2 * layers, 1, LANES), F32),
                vmem((2, 1, LANES), F32),
                vmem((2, blocks // 2, 1, LANES), F32),
                dma((7,)),
                dma((4, 2)),
                dma((2, 2)),
                dma((2, 2)),
                dma((2, 2)),
                dma((2, 2)),
            ],
            compiler_params=pltpu.CompilerParams(
                collective_id=0, has_side_effects=True, vmem_limit_bytes=32 << 20
            ),
        )(
            *(
                pltpu.with_memory_space_constraint(value, pltpu.HBM)
                for value in (
                    flat,
                    inverse,
                    coupling,
                    operator,
                    face_ids.T,
                    orientation.T,
                    scale.reshape(1, ELEMENTS),
                )
            )
        )
        interior, sides, tops = pl.pallas_call(
            combine,
            out_shape=(shapes[0], shapes[3], shapes[5]),
            in_specs=[local] * 8,
            out_specs=(local,) * 3,
            compiler_params=pltpu.CompilerParams(vmem_limit_bytes=16 << 20),
        )(weights, *found)
        return (
            interior.reshape(RIGHT, ELEMENTS, NODES).transpose(2, 0, 1),
            sides.reshape(64, RIGHT, 128),
            tops.reshape(64, RIGHT, ELEMENTS),
        )

    columns = P(None, None, ("gz", "dev"))
    return jax.shard_map(
        per_device,
        mesh=mesh,
        in_specs=(
            columns,
            P(),
            P(),
            P(),
            P(("gz", "dev"), None),
            P(("gz", "dev"), None),
            P(("gz", "dev")),
        ),
        out_specs=(columns, columns, columns),
        check_vma=False,
    )
```

```python
import functools

import jax
import jax.numpy as jnp
from jax import lax
from jax.experimental import pallas as pl
from jax.experimental.pallas import tpu as pltpu
from jax.sharding import PartitionSpec as P

MESH = pl.DeviceIdType.MESH
F32 = jnp.float32
BF16 = jnp.bfloat16
LANES = 128
ELEMENTS = 64
RIGHT = 8
NODES = 512
LOCAL = 384
ROWS = RIGHT * ELEMENTS
PAIRS = RIGHT // 2


def turns(layers, blocks):
    def ring(step, count):
        return min(step, count - step)

    deep = blocks // 8
    steps = [
        (x, z, y, core)
        for x in range(layers)
        for z in range(deep)
        for y in range(4)
        for core in (1, 0)
        if (x, z, y, core) != (0, 0, 0, 0)
    ]
    return sorted(
        steps, key=lambda step: (-ring(step[0], layers) - ring(step[1], deep) - ring(step[2], 4), step[3])
    )


def halves(value):
    high = value.astype(BF16)
    return high, (value - high.astype(F32)).astype(BF16)


def dot(left, right):
    return jnp.dot(left, right, preferred_element_type=F32)


def dot_three(left_high, left_low, right_high, right_low):
    return dot(left_high, right_high) + (dot(left_high, right_low) + dot(left_low, right_high))


def twice(onehot):
    return jnp.concatenate([onehot, onehot], axis=1)


def pick(onehots, value):
    return dot(onehots, jnp.concatenate(halves(value), axis=0))


def lane_of(shape):
    return lax.broadcasted_iota(jnp.int32, shape, 1)


def row_of(shape):
    return lax.broadcasted_iota(jnp.int32, shape, 0)


def swap_pair(first, second):
    low = lane_of(first.shape) < 64
    return (
        jnp.where(low, first, pltpu.roll(second, 64, 1)),
        jnp.where(low, pltpu.roll(first, 64, 1), second),
    )


def turned(value, index):
    return jnp.take_along_axis(value, index, axis=1, mode="promise_in_bounds")


def kernel(
    layers,
    blocks,
    source_hbm,
    inverse_hbm,
    coupling_hbm,
    operator_hbm,
    faces_hbm,
    codes_hbm,
    scale_hbm,
    solved,
    moved_zero,
    moved_one,
    sides_zero,
    sides_one,
    tops_zero,
    tops_one,
    weights,
    source,
    inverse,
    coupling,
    operator,
    faces_ref,
    codes_ref,
    scale_ref,
    source_h,
    source_l,
    inverse_h,
    inverse_l,
    coupling_h,
    coupling_l,
    operator_hh,
    operator_l,
    merged_h,
    merged_l,
    merged_thh,
    merged_tl,
    table,
    index_to,
    index_from,
    scales,
    first,
    image,
    update,
    vector,
    slots_first,
    slots_second,
    bottoms,
    tops,
    second_image,
    sent,
    received,
    got_bottoms,
    got_tops,
    near_out,
    near_in,
    far_out,
    far_in,
    load_sem,
    swap_sem,
    up_sem,
    down_sem,
    near_sem,
    far_sem,
):
    layer = lax.axis_index("gz")
    me = lax.axis_index("dev")
    others = blocks - 1
    core = me % 2

    deep = blocks // 8
    along_x = [(layer + step) % layers for step in range(layers)]
    along_z = [(me // 8 + step) % deep * 8 for step in range(deep)]
    along_y = [(me % 8 // 2 + step) % 4 * 2 for step in range(4)]
    along_core = [core, 1 - core]
    everyone = [
        (x, z, y, c, along_x[x], along_z[z] + along_y[y] + along_core[c])
        for x, z, y, c in turns(layers, blocks)
    ]
    peers = [peer for x, *_, peer in everyone if x == 0]
    column_peers = [(at, peer) for x, z, y, _, at, peer in everyone if z == 0 and y == 0]
    far_peers = [peer for x, _, _, c, _, peer in everyone if x == 0 and c == 0]

    barrier = pltpu.get_barrier_semaphore()
    for peer in peers:
        pl.semaphore_signal(barrier, inc=1, device_id=(layer, peer), device_id_type=MESH)
    for at, peer in column_peers:
        if at is not along_x[0]:
            pl.semaphore_signal(barrier, inc=1, device_id=(at, peer), device_id_type=MESH)

    loads = [
        pltpu.make_async_copy(inverse_hbm, inverse, load_sem.at[0]),
        pltpu.make_async_copy(coupling_hbm, coupling, load_sem.at[1]),
        pltpu.make_async_copy(source_hbm, source, load_sem.at[2]),
        pltpu.make_async_copy(operator_hbm, operator, load_sem.at[3]),
        pltpu.make_async_copy(faces_hbm, faces_ref, load_sem.at[4]),
        pltpu.make_async_copy(codes_hbm, codes_ref, load_sem.at[5]),
        pltpu.make_async_copy(scale_hbm, scale_ref, load_sem.at[6]),
    ]
    for load in loads[4:] + loads[:4]:
        load.start()

    here = pl.ds(pl.multiple_of(me * 8, 8), 8)
    for phase in range(5):
        received[phase, here, :] = jnp.zeros((8, LANES), F32)

    @pl.when(layer == 0)
    def _():
        got_bottoms[...] = jnp.zeros(got_bottoms.shape, F32)

    @pl.when(layer == layers - 1)
    def _():
        got_tops[...] = jnp.zeros(got_tops.shape, F32)

    table[...] = jnp.zeros(table.shape, F32)
    for load in loads[4:]:
        load.wait()
    faces = faces_ref[...].astype(F32)
    codes = codes_ref[...].astype(F32)
    for row in range(2):
        table[row : row + 1, 0:64] = faces[2 * row : 2 * row + 1]
        table[row : row + 1, 64:128] = faces[2 * row + 1 : 2 * row + 2]
    for row in range(3):
        table[2 + row : 3 + row, 0:64] = codes[2 * row : 2 * row + 1]
        table[2 + row : 3 + row, 64:128] = codes[2 * row + 1 : 2 * row + 2]
    table[5:6, 0:64] = scale_ref[...].astype(F32)
    columns = jnp.transpose(table[...])
    square = (LANES, LANES)
    first_row = jnp.broadcast_to(table[0:1, :], square).astype(jnp.int32) - me * LANES
    second_row = jnp.broadcast_to(table[1:2, :], square).astype(jnp.int32)
    first_col = jnp.broadcast_to(columns[:, 0:1], square).astype(jnp.int32) - me * LANES
    second_col = jnp.broadcast_to(columns[:, 1:2], square).astype(jnp.int32)

    def onehot(condition):
        return jnp.where(condition, 1.0, 0.0).astype(F32)

    near = twice(onehot(first_col + me * LANES == second_row).astype(BF16))
    near_back = twice(onehot(first_row + me * LANES == second_col).astype(BF16))
    into_faces = twice(onehot(first_row == row_of(square)).astype(BF16))
    peer_shape = (blocks, LANES)
    owner_row = second_row[:blocks] // LANES
    peer_row = row_of(peer_shape)
    to_owner_f = onehot((owner_row == peer_row) & (peer_row != me))
    to_owner = twice(to_owner_f.astype(BF16))
    from_owner = twice(jnp.transpose(to_owner_f).astype(BF16))
    slot_number = (second_row[:blocks] % LANES + 1).astype(F32)
    named = jnp.sum(to_owner_f * slot_number, axis=1, keepdims=True)
    sent[3, pl.ds(0, blocks, stride=8), :] = jnp.broadcast_to(named, peer_shape)

    lane = lane_of((ELEMENTS, LANES))
    low = lane < 64
    node_a, node_b = lane % 64 // 8, lane % 8
    for chunk in range(3):
        code = jnp.where(
            low,
            jnp.broadcast_to(columns[0:64, 2 + chunk : 3 + chunk], lane.shape),
            jnp.broadcast_to(columns[64:128, 2 + chunk : 3 + chunk], lane.shape),
        ).astype(jnp.int32)
        swapped, flip_a, flip_b = code // 4 % 2 == 1, code // 2 % 2 == 1, code % 2 == 1
        half = lane // 64 * 64
        a = jnp.where(flip_a, 7 - node_a, node_a)
        b = jnp.where(flip_b, 7 - node_b, node_b)
        index_to[chunk] = half + jnp.where(swapped, b * 8 + a, a * 8 + b)
        a = jnp.where(swapped, node_b, node_a)
        b = jnp.where(swapped, node_a, node_b)
        index_from[chunk] = half + jnp.where(flip_a, 7 - a, a) * 8 + jnp.where(flip_b, 7 - b, b)
    scales[...] = jnp.broadcast_to(columns[0:64, 5:6], scales.shape)
    live = (low & (layer > 0)) | ((lane >= 64) & (layer < layers - 1))

    def rows_of(right):
        return slice(right * ELEMENTS, (right + 1) * ELEMENTS)

    def lanes_of(chunk):
        return slice(chunk * LANES, (chunk + 1) * LANES)

    loads[0].wait()
    inverse_h[...], inverse_l[...] = halves(inverse[...])
    loads[1].wait()
    coupling_h[...], coupling_l[...] = halves(coupling[...])
    merged = dot_three(inverse_h[...], inverse_l[...], coupling_h[...], coupling_l[...])
    merged_h[...], merged_l[...] = halves(merged)
    loads[2].wait()
    source_h[...], source_l[...] = halves(source[...])
    image[...] = dot_three(source_h[...], source_l[...], merged_h[...], merged_l[...])

    def to_slots(vector, chunks, stores):
        for chunk in chunks:
            for pair in range(PAIRS):
                left = turned(vector[rows_of(2 * pair), lanes_of(chunk)], index_from[chunk])
                right = turned(vector[rows_of(2 * pair + 1), lanes_of(chunk)], index_from[chunk])
                stores[chunk](pair, *swap_pair(left, right))

    def store_slots(ref):
        def store(pair, even, odd):
            ref[0:64, lanes_of(pair)] = even
            ref[64:128, lanes_of(pair)] = odd

        return store

    def store_ends(pair, even, odd):
        bottoms[rows_of(pair), :] = even
        tops[rows_of(pair), :] = odd

    stores = (store_slots(slots_first), store_slots(slots_second), store_ends)

    def wait_rows(ref, rows, sem):
        whole = ref.at[pl.ds(0, rows)]
        pltpu.make_async_copy(whole, whole, sem).wait()

    def up_copy(phase):
        return pltpu.make_async_remote_copy(
            tops,
            got_bottoms.at[phase],
            up_sem.at[phase, 0],
            up_sem.at[phase, 1],
            device_id={"gz": layer + 1},
            device_id_type=MESH,
        )

    def down_copy(phase):
        return pltpu.make_async_remote_copy(
            bottoms,
            got_tops.at[phase],
            down_sem.at[phase, 0],
            down_sem.at[phase, 1],
            device_id={"gz": layer - 1},
            device_id_type=MESH,
        )

    def start_ends(phase):
        @pl.when(layer < layers - 1)
        def _():
            up_copy(phase).start()

        @pl.when(layer > 0)
        def _():
            down_copy(phase).start()

    def finish_ends(phase):
        @pl.when(layer < layers - 1)
        def _():
            up_copy(phase).wait_send()
            down_copy(phase).wait_recv()

        @pl.when(layer > 0)
        def _():
            down_copy(phase).wait_send()
            up_copy(phase).wait_recv()

    def send_rows(phase, rows):
        for peer in peers:
            pltpu.make_async_remote_copy(
                sent.at[phase, pl.ds(pl.multiple_of(peer * 8, 8), rows)],
                received.at[phase, pl.ds(pl.multiple_of(me * 8, 8), rows)],
                swap_sem.at[phase, 0],
                swap_sem.at[phase, 1],
                device_id=(layer, peer),
                device_id_type=MESH,
            ).start()

    def wait_sent(phase, rows):
        wait_rows(sent.at[phase], others * rows, swap_sem.at[phase, 0])

    def wait_received(phase, rows):
        wait_rows(received.at[phase], others * rows, swap_sem.at[phase, 1])

    def put(phase, first_row, value):
        for pair in range(PAIRS):
            sent[phase, pl.ds(first_row + pair, blocks, stride=8), :] = value[:, lanes_of(pair)]

    def got(phase, row):
        return received[phase, pl.ds(row, blocks, stride=8), :]

    def arrivals(chunk, pair, value):
        for offset, part in enumerate(swap_pair(value[0:64], value[64:128])):
            yield 2 * pair + offset, turned(part, index_to[chunk])

    def end_arrivals(phase):
        for pair in range(PAIRS):
            ends = got_bottoms[phase, rows_of(pair), :], got_tops[phase, rows_of(pair), :]
            for right, part in arrivals(2, pair, jnp.concatenate(ends, axis=0)):
                spot = rows_of(right), lanes_of(2)
                yield spot, jnp.where(live, image[spot] + part, 0.0)

    def keep(ref, spot, value):
        rows, lanes = spot
        ref[spot] = value
        high, low_part = halves(value)
        vector[rows, 2 * lanes.start : 2 * lanes.start + LANES] = high
        vector[rows, 2 * lanes.start + LANES : 2 * lanes.stop] = low_part

    def summed(quantities):
        lanes = lane_of((RIGHT, LANES))
        place = row_of((RIGHT, LANES))
        spread = jnp.zeros((RIGHT, LANES), F32)
        for number, rows in enumerate(quantities):
            total = jnp.sum(jnp.concatenate(rows, axis=0), axis=1, keepdims=True)
            spread = jnp.where(lanes == place + number * RIGHT, total, spread)
        return jnp.sum(spread, axis=0, keepdims=True)

    def share(mine, out_ref, in_ref, place, sem, targets):
        out_ref[...] = mine
        in_ref[place] = mine
        for at, peer in targets:
            pltpu.make_async_remote_copy(
                out_ref,
                in_ref.at[place],
                sem.at[0],
                sem.at[1],
                device_id=(at, peer),
                device_id_type=MESH,
            ).start()

    def shared(in_ref, sem, count):
        wait_rows(in_ref, count, sem.at[1])
        wait_rows(in_ref, count, sem.at[0])
        return jnp.sum(in_ref[...], axis=0)

    def share_near(phase, quantities):
        share(
            summed(quantities),
            near_out.at[phase],
            near_in.at[phase],
            layer * 2 + core,
            near_sem.at[phase],
            column_peers,
        )

    def share_far(phase):
        share(
            shared(near_in.at[phase], near_sem.at[phase], len(column_peers)),
            far_out.at[phase],
            far_in.at[phase],
            me // 2,
            far_sem.at[phase],
            [(layer, peer) for peer in far_peers],
        )

    def columns_of(row, count):
        total = jnp.broadcast_to(row, (RIGHT, LANES))
        lanes = lane_of((RIGHT, LANES))
        place = row_of((RIGHT, LANES))
        return [
            jnp.broadcast_to(
                jnp.sum(
                    jnp.where(lanes == place + number * RIGHT, total, 0.0), axis=1, keepdims=True
                ),
                (RIGHT, LANES),
            )
            for number in range(count)
        ]

    def finish_far(phase, count):
        return columns_of(shared(far_in.at[phase], far_sem.at[phase], len(far_peers)), count)

    def owned_square(values):
        kept = values[0] * values[0] + jnp.where(low, 0.0, values[2] * values[2])
        return jnp.sum(kept, axis=0, keepdims=True)

    def inner_rows(left, right):
        kept = left[0] * right[0] + left[1] * right[1] + left[2] * right[2]
        return jnp.sum(kept, axis=0, keepdims=True)

    def chunks_of(ref, right):
        return [ref[rows_of(right), lanes_of(chunk)] for chunk in range(3)]

    def stacked(chunk):
        return slice(2 * chunk * LANES, 2 * (chunk + 1) * LANES)

    def applied(double_ref, low_ref, chunks):
        return sum(
            dot(vector[:, stacked(chunk)], double_ref[stacked(chunk), :])
            + dot(
                vector[:, 2 * chunk * LANES : (2 * chunk + 1) * LANES], low_ref[lanes_of(chunk), :]
            )
            for chunk in chunks
        )

    def hold(double_ref, low_ref, value):
        high, low_part = halves(value)
        low_ref[...] = low_part
        for chunk in range(3):
            double_ref[stacked(chunk), :] = jnp.concatenate([high[lanes_of(chunk)]] * 2, axis=0)

    def face_values(vector, sides_ref, tops_ref):
        for pair in range(PAIRS):
            for chunk in (0, 2):
                left = turned(vector[rows_of(2 * pair), lanes_of(chunk)], index_from[chunk])
                right = turned(vector[rows_of(2 * pair + 1), lanes_of(chunk)], index_from[chunk])
                even, odd = swap_pair(left, right)
                if chunk == 0:
                    turned_back = jnp.transpose(
                        pick(into_faces, jnp.concatenate([even, odd], axis=0))
                    )
                    target = sides_ref
                else:
                    turned_back = jnp.transpose(odd)
                    target = tops_ref
                for offset in range(2):
                    target[pl.ds(2 * pair + offset, 64, stride=8), :] = turned_back[
                        offset * 64 : (offset + 1) * 64
                    ]

    to_slots(image, (2, 1, 0), stores)
    put(0, 0, pick(to_owner, slots_second[...]))
    pl.semaphore_wait(barrier, others + 2 * (layers - 1))

    send_rows(3, 1)
    send_rows(0, 4)
    start_ends(0)
    solved[...] = dot_three(source_h[...], source_l[...], inverse_h[...], inverse_l[...])
    loads[3].wait()
    hold(operator_hh, operator_l, operator[...])
    for right in range(RIGHT):
        for part in range(4):
            solved[rows_of(right), lanes_of(part)] = solved[rows_of(right), lanes_of(part)] / scales[...]
    hold(merged_thh, merged_tl, jnp.transpose(merged_h[...].astype(F32) + merged_l[...].astype(F32)))
    nearby_first = pick(near, slots_second[...])
    wait_received(3, 1)
    to_holder_f = onehot(got(3, 0).astype(jnp.int32) == first_row[:blocks] + 1)
    to_holder = twice(to_holder_f.astype(BF16))
    from_holder = twice(jnp.transpose(to_holder_f).astype(BF16))

    put(1, 0, pick(to_holder, slots_first[...]))
    send_rows(1, 4)
    wait_received(0, 4)
    for pair in range(PAIRS):
        value = nearby_first[:, lanes_of(pair)] + pick(from_holder, got(0, pair))
        for right, part in arrivals(0, pair, value):
            spot = rows_of(right), lanes_of(0)
            keep(first, spot, image[spot] + part)
    finish_ends(0)
    for spot, value in end_arrivals(0):
        keep(first, spot, value)
    second_image[...] = applied(operator_hh, operator_l, (0, 2))
    nearby_second = pick(near_back, slots_first[...])
    wait_received(1, 4)
    for pair in range(PAIRS):
        value = nearby_second[:, lanes_of(pair)] + pick(from_owner, got(1, pair))
        for right, part in arrivals(1, pair, value):
            spot = rows_of(right), lanes_of(1)
            keep(first, spot, image[spot] + part)
    image[...] = second_image[...] + applied(operator_hh, operator_l, (1,))

    squares, curves = [], []
    for right in range(RIGHT):
        for chunk in range(3):
            image[rows_of(right), lanes_of(chunk)] = image[rows_of(right), lanes_of(chunk)] * scales[...]
        mine = chunks_of(first, right)
        squares.append(owned_square(mine))
        curves.append(inner_rows(mine, chunks_of(image, right)))
    share_near(0, [squares, curves])
    wait_sent(3, 1)
    wait_sent(0, 4)
    wait_sent(1, 4)
    to_slots(image, (1, 0, 2), stores)
    put(2, 0, pick(to_owner, slots_second[...]))
    send_rows(2, 4)
    put(4, 0, pick(to_holder, slots_first[...]))
    send_rows(4, 4)
    start_ends(1)

    nearby_first = pick(near, slots_second[...])
    nearby_second = pick(near_back, slots_first[...])
    moved_zero[...] = applied(merged_thh, merged_tl, (0, 1, 2))
    face_values(first, sides_zero, tops_zero)
    share_far(0)
    finish_ends(1)
    for spot, value in end_arrivals(1):
        keep(update, spot, value)
    wait_received(2, 4)
    for pair in range(PAIRS):
        value = nearby_first[:, lanes_of(pair)] + pick(from_holder, got(2, pair))
        for right, part in arrivals(0, pair, value):
            spot = rows_of(right), lanes_of(0)
            keep(update, spot, image[spot] + part)
    second_image[...] = applied(operator_hh, operator_l, (0, 2))
    wait_received(4, 4)
    for pair in range(PAIRS):
        value = nearby_second[:, lanes_of(pair)] + pick(from_owner, got(4, pair))
        for right, part in arrivals(1, pair, value):
            spot = rows_of(right), lanes_of(1)
            keep(update, spot, image[spot] + part)
    second_image[...] = second_image[...] + applied(operator_hh, operator_l, (1,))
    wait_sent(2, 4)
    wait_sent(4, 4)

    norm, curve = finish_far(0, 2)
    alpha = norm / curve
    squares, crosses, curves = [], [], []
    for right in range(RIGHT):
        step = alpha[right : right + 1, :]
        before, change = chunks_of(first, right), chunks_of(update, right)
        old, turned_change = chunks_of(image, right), chunks_of(second_image, right)
        mine = [before[chunk] - step * change[chunk] for chunk in range(3)]
        new = [old[chunk] - step * (turned_change[chunk] * scales[...]) for chunk in range(3)]
        squares.append(owned_square(mine))
        crosses.append(inner_rows(mine, old))
        curves.append(inner_rows(mine, new))
    share_near(1, [squares, crosses, curves])

    moved_one[...] = applied(merged_thh, merged_tl, (0, 1, 2))
    share_far(1)
    face_values(update, sides_one, tops_one)
    norm_next, cross, curve_next = finish_far(1, 3)
    beta = norm_next / norm
    curve_next = curve_next + 2.0 * beta * cross + beta * beta * curve
    weight_update = norm_next / curve_next
    weights[0:8, :] = alpha + weight_update * beta + weight_update
    weights[8:16, :] = weight_update * alpha


def combine(
    weights,
    solved,
    moved_zero,
    moved_one,
    sides_zero,
    sides_one,
    tops_zero,
    tops_one,
    interior_hbm,
    sides_hbm,
    tops_hbm,
    interior,
    sides,
    tops,
    sem,
):
    writes = []

    def write(here, there, rows):
        writes.append(pltpu.make_async_copy(here.at[rows], there.at[rows], sem.at[len(writes)]))
        writes[-1].start()

    for right in range(RIGHT):
        rows = slice(right * 64, right * 64 + 64)
        for part in range(4):
            spot = rows, slice(part * LANES, part * LANES + LANES)
            interior[spot] = (
                solved[spot]
                - weights[right : right + 1, :] * moved_zero[spot]
                + weights[8 + right : 9 + right, :] * moved_one[spot]
            )
        if right % 2 == 1:
            write(interior, interior_hbm, pl.ds(right * 64 - 64, 128))
    for node in range(64):
        spot = slice(node * 8, node * 8 + 8)
        sides[spot, :] = weights[0:8, :] * sides_zero[spot, :] - weights[8:16, :] * sides_one[spot, :]
        tops[spot, :] = weights[0:8, :64] * tops_zero[spot, :] - weights[8:16, :64] * tops_one[spot, :]
    write(sides, sides_hbm, pl.ds(0, 512))
    write(tops, tops_hbm, pl.ds(0, 512))
    for started in writes:
        started.wait()


def solution(mesh):
    layers, blocks = mesh.shape["gz"], mesh.shape["dev"]

    def per_device(source, inverse, coupling, operator, face_ids, orientation, scale):
        flat = source.transpose(1, 2, 0).reshape(ROWS, NODES)
        vmem = pltpu.VMEM
        far = pl.BlockSpec(memory_space=pltpu.HBM)
        local = pl.BlockSpec(memory_space=pltpu.VMEM)
        dma = pltpu.SemaphoreType.DMA
        shapes = [
            *[jax.ShapeDtypeStruct((ROWS, NODES), F32)] * 3,
            *[jax.ShapeDtypeStruct((512, 128), F32)] * 2,
            *[jax.ShapeDtypeStruct((512, 64), F32)] * 2,
            jax.ShapeDtypeStruct((16, LANES), F32),
        ]
        *found, weights = pl.pallas_call(
            functools.partial(kernel, layers, blocks),
            out_shape=tuple(shapes),
            in_specs=[far] * 7,
            out_specs=(local,) * 8,
            scratch_shapes=[
                vmem((ROWS, NODES), F32),
                vmem((NODES, NODES), F32),
                vmem((NODES, LOCAL), F32),
                vmem((LOCAL, LOCAL), F32),
                vmem((4, ELEMENTS), jnp.int32),
                vmem((6, ELEMENTS), jnp.int32),
                vmem((1, ELEMENTS), jnp.int32),
                *[vmem((ROWS, NODES), BF16)] * 2,
                *[vmem((NODES, NODES), BF16)] * 2,
                *[vmem((NODES, LOCAL), BF16)] * 2,
                vmem((2 * LOCAL, LOCAL), BF16),
                vmem((LOCAL, LOCAL), BF16),
                *[vmem((NODES, LOCAL), BF16)] * 2,
                vmem((2 * LOCAL, NODES), BF16),
                vmem((LOCAL, NODES), BF16),
                vmem((LANES, LANES), F32),
                vmem((3, ELEMENTS, LANES), jnp.int32),
                vmem((3, ELEMENTS, LANES), jnp.int32),
                vmem((ELEMENTS, LANES), F32),
                *[vmem((ROWS, LOCAL), F32)] * 3,
                vmem((ROWS, 2 * LOCAL), BF16),
                *[vmem((128, 512), F32)] * 2,
                *[vmem((256, 128), F32)] * 2,
                vmem((ROWS, LOCAL), F32),
                *[vmem((5, blocks * 8, LANES), F32)] * 2,
                *[vmem((2, 256, 128), F32)] * 2,
                vmem((2, 1, LANES), F32),
                vmem((2, 2 * layers, 1, LANES), F32),
                vmem((2, 1, LANES), F32),
                vmem((2, blocks // 2, 1, LANES), F32),
                dma((7,)),
                dma((5, 2)),
                dma((2, 2)),
                dma((2, 2)),
                dma((2, 2)),
                dma((2, 2)),
            ],
            compiler_params=pltpu.CompilerParams(
                collective_id=0, has_side_effects=True, vmem_limit_bytes=32 << 20
            ),
        )(
            *(
                pltpu.with_memory_space_constraint(value, pltpu.HBM)
                for value in (
                    flat,
                    inverse,
                    coupling,
                    operator,
                    face_ids.T,
                    orientation.T,
                    scale.reshape(1, ELEMENTS),
                )
            )
        )
        interior, sides, tops = pl.pallas_call(
            combine,
            out_shape=(shapes[0], shapes[3], shapes[5]),
            in_specs=[local] * 8,
            out_specs=(pl.BlockSpec(memory_space=pl.ANY),) * 3,
            scratch_shapes=[
                vmem((ROWS, NODES), F32),
                vmem((512, 128), F32),
                vmem((512, 64), F32),
                dma((6,)),
            ],
            compiler_params=pltpu.CompilerParams(vmem_limit_bytes=16 << 20),
        )(weights, *found)
        return (
            interior.reshape(RIGHT, ELEMENTS, NODES).transpose(2, 0, 1),
            sides.reshape(64, RIGHT, 128),
            tops.reshape(64, RIGHT, ELEMENTS),
        )

    columns = P(None, None, ("gz", "dev"))
    return jax.shard_map(
        per_device,
        mesh=mesh,
        in_specs=(
            columns,
            P(),
            P(),
            P(),
            P(("gz", "dev"), None),
            P(("gz", "dev"), None),
            P(("gz", "dev")),
        ),
        out_specs=(columns, columns, columns),
        check_vma=False,
    )
```

```python
import functools

import jax
import jax.numpy as jnp
from jax import lax
from jax.experimental import pallas as pl
from jax.experimental.pallas import tpu as pltpu
from jax.sharding import PartitionSpec as P

MESH = pl.DeviceIdType.MESH
F32 = jnp.float32
BF16 = jnp.bfloat16
LANES = 128
ELEMENTS = 64
RIGHT = 8
NODES = 512
LOCAL = 384
ROWS = RIGHT * ELEMENTS
PAIRS = RIGHT // 2


def turns(layers, blocks):
    def ring(step, count):
        return min(step, count - step)

    deep = blocks // 8
    steps = [
        (x, z, y, core)
        for x in range(layers)
        for z in range(deep)
        for y in range(4)
        for core in (1, 0)
        if (x, z, y, core) != (0, 0, 0, 0)
    ]
    return sorted(
        steps, key=lambda step: (-ring(step[0], layers) - ring(step[1], deep) - ring(step[2], 4), step[3])
    )


def halves(value):
    high = value.astype(BF16)
    return high, (value - high.astype(F32)).astype(BF16)


def dot(left, right):
    return jnp.dot(left, right, preferred_element_type=F32)


def dot_three(left_high, left_low, right_high, right_low):
    return dot(left_high, right_high) + (dot(left_high, right_low) + dot(left_low, right_high))


def twice(onehot):
    return jnp.concatenate([onehot, onehot], axis=1)


def pick(onehots, value):
    return dot(onehots, jnp.concatenate(halves(value), axis=0))


def lane_of(shape):
    return lax.broadcasted_iota(jnp.int32, shape, 1)


def row_of(shape):
    return lax.broadcasted_iota(jnp.int32, shape, 0)


def swap_pair(first, second):
    low = lane_of(first.shape) < 64
    return (
        jnp.where(low, first, pltpu.roll(second, 64, 1)),
        jnp.where(low, pltpu.roll(first, 64, 1), second),
    )


def turned(value, index):
    return jnp.take_along_axis(value, index, axis=1, mode="promise_in_bounds")


def kernel(
    layers,
    blocks,
    source_hbm,
    inverse_hbm,
    coupling_hbm,
    operator_hbm,
    faces_hbm,
    codes_hbm,
    scale_hbm,
    solved,
    moved_zero,
    moved_one,
    sides_zero,
    sides_one,
    tops_zero,
    tops_one,
    weights,
    source,
    inverse,
    coupling,
    operator,
    faces_ref,
    codes_ref,
    scale_ref,
    source_h,
    source_l,
    inverse_h,
    inverse_l,
    coupling_h,
    coupling_l,
    operator_hh,
    operator_l,
    merged_h,
    merged_l,
    merged_thh,
    merged_tl,
    table,
    index_to,
    index_from,
    scales,
    first,
    image,
    update,
    vector,
    slots_first,
    slots_second,
    bottoms,
    tops,
    second_image,
    sent,
    received,
    got_bottoms,
    got_tops,
    near_out,
    near_in,
    far_out,
    far_in,
    pair_out,
    pair_in,
    all_out,
    all_in,
    load_sem,
    swap_sem,
    up_sem,
    down_sem,
    near_sem,
    far_sem,
    pair_sem,
    all_sem,
):
    layer = lax.axis_index("gz")
    me = lax.axis_index("dev")
    others = blocks - 1
    core = me % 2

    deep = blocks // 8
    along_x = [(layer + step) % layers for step in range(layers)]
    along_z = [(me // 8 + step) % deep * 8 for step in range(deep)]
    along_y = [(me % 8 // 2 + step) % 4 * 2 for step in range(4)]
    along_core = [core, 1 - core]
    everyone = [
        (x, z, y, c, along_x[x], along_z[z] + along_y[y] + along_core[c])
        for x, z, y, c in turns(layers, blocks)
    ]
    peers = [peer for x, *_, peer in everyone if x == 0]
    column_peers = [(at, peer) for x, z, y, _, at, peer in everyone if z == 0 and y == 0]
    far_peers = [peer for x, _, _, c, _, peer in everyone if x == 0 and c == 0]

    barrier = pltpu.get_barrier_semaphore()
    for peer in peers:
        pl.semaphore_signal(barrier, inc=1, device_id=(layer, peer), device_id_type=MESH)
    for at, peer in column_peers:
        if at is not along_x[0]:
            pl.semaphore_signal(barrier, inc=1, device_id=(at, peer), device_id_type=MESH)

    loads = [
        pltpu.make_async_copy(inverse_hbm, inverse, load_sem.at[0]),
        pltpu.make_async_copy(coupling_hbm, coupling, load_sem.at[1]),
        pltpu.make_async_copy(source_hbm, source, load_sem.at[2]),
        pltpu.make_async_copy(operator_hbm, operator, load_sem.at[3]),
        pltpu.make_async_copy(faces_hbm, faces_ref, load_sem.at[4]),
        pltpu.make_async_copy(codes_hbm, codes_ref, load_sem.at[5]),
        pltpu.make_async_copy(scale_hbm, scale_ref, load_sem.at[6]),
    ]
    for load in loads[4:] + loads[:4]:
        load.start()

    here = pl.ds(pl.multiple_of(me * 8, 8), 8)
    for phase in range(5):
        received[phase, here, :] = jnp.zeros((8, LANES), F32)

    @pl.when(layer == 0)
    def _():
        got_bottoms[...] = jnp.zeros(got_bottoms.shape, F32)

    @pl.when(layer == layers - 1)
    def _():
        got_tops[...] = jnp.zeros(got_tops.shape, F32)

    table[...] = jnp.zeros(table.shape, F32)
    for load in loads[4:]:
        load.wait()
    faces = faces_ref[...].astype(F32)
    codes = codes_ref[...].astype(F32)
    for row in range(2):
        table[row : row + 1, 0:64] = faces[2 * row : 2 * row + 1]
        table[row : row + 1, 64:128] = faces[2 * row + 1 : 2 * row + 2]
    for row in range(3):
        table[2 + row : 3 + row, 0:64] = codes[2 * row : 2 * row + 1]
        table[2 + row : 3 + row, 64:128] = codes[2 * row + 1 : 2 * row + 2]
    table[5:6, 0:64] = scale_ref[...].astype(F32)
    columns = jnp.transpose(table[...])
    square = (LANES, LANES)
    first_row = jnp.broadcast_to(table[0:1, :], square).astype(jnp.int32) - me * LANES
    second_row = jnp.broadcast_to(table[1:2, :], square).astype(jnp.int32)
    first_col = jnp.broadcast_to(columns[:, 0:1], square).astype(jnp.int32) - me * LANES
    second_col = jnp.broadcast_to(columns[:, 1:2], square).astype(jnp.int32)

    def onehot(condition):
        return jnp.where(condition, 1.0, 0.0).astype(F32)

    near = twice(onehot(first_col + me * LANES == second_row).astype(BF16))
    near_back = twice(onehot(first_row + me * LANES == second_col).astype(BF16))
    into_faces = twice(onehot(first_row == row_of(square)).astype(BF16))
    peer_shape = (blocks, LANES)
    owner_row = second_row[:blocks] // LANES
    peer_row = row_of(peer_shape)
    to_owner_f = onehot((owner_row == peer_row) & (peer_row != me))
    to_owner = twice(to_owner_f.astype(BF16))
    from_owner = twice(jnp.transpose(to_owner_f).astype(BF16))
    slot_number = (second_row[:blocks] % LANES + 1).astype(F32)
    named = jnp.sum(to_owner_f * slot_number, axis=1, keepdims=True)
    sent[3, pl.ds(0, blocks, stride=8), :] = jnp.broadcast_to(named, peer_shape)

    lane = lane_of((ELEMENTS, LANES))
    low = lane < 64
    node_a, node_b = lane % 64 // 8, lane % 8
    for chunk in range(3):
        code = jnp.where(
            low,
            jnp.broadcast_to(columns[0:64, 2 + chunk : 3 + chunk], lane.shape),
            jnp.broadcast_to(columns[64:128, 2 + chunk : 3 + chunk], lane.shape),
        ).astype(jnp.int32)
        swapped, flip_a, flip_b = code // 4 % 2 == 1, code // 2 % 2 == 1, code % 2 == 1
        half = lane // 64 * 64
        a = jnp.where(flip_a, 7 - node_a, node_a)
        b = jnp.where(flip_b, 7 - node_b, node_b)
        index_to[chunk] = half + jnp.where(swapped, b * 8 + a, a * 8 + b)
        a = jnp.where(swapped, node_b, node_a)
        b = jnp.where(swapped, node_a, node_b)
        index_from[chunk] = half + jnp.where(flip_a, 7 - a, a) * 8 + jnp.where(flip_b, 7 - b, b)
    scales[...] = jnp.broadcast_to(columns[0:64, 5:6], scales.shape)
    live = (low & (layer > 0)) | ((lane >= 64) & (layer < layers - 1))

    def rows_of(right):
        return slice(right * ELEMENTS, (right + 1) * ELEMENTS)

    def lanes_of(chunk):
        return slice(chunk * LANES, (chunk + 1) * LANES)

    loads[0].wait()
    inverse_h[...], inverse_l[...] = halves(inverse[...])
    loads[1].wait()
    coupling_h[...], coupling_l[...] = halves(coupling[...])
    merged = dot_three(inverse_h[...], inverse_l[...], coupling_h[...], coupling_l[...])
    merged_h[...], merged_l[...] = halves(merged)
    loads[2].wait()
    source_h[...], source_l[...] = halves(source[...])
    image[...] = dot_three(source_h[...], source_l[...], merged_h[...], merged_l[...])

    def to_slots(vector, chunks, stores):
        for chunk in chunks:
            for pair in range(PAIRS):
                left = turned(vector[rows_of(2 * pair), lanes_of(chunk)], index_from[chunk])
                right = turned(vector[rows_of(2 * pair + 1), lanes_of(chunk)], index_from[chunk])
                stores[chunk](pair, *swap_pair(left, right))

    def store_slots(ref):
        def store(pair, even, odd):
            ref[0:64, lanes_of(pair)] = even
            ref[64:128, lanes_of(pair)] = odd

        return store

    def store_ends(pair, even, odd):
        bottoms[rows_of(pair), :] = even
        tops[rows_of(pair), :] = odd

    stores = (store_slots(slots_first), store_slots(slots_second), store_ends)

    def wait_rows(ref, rows, sem):
        whole = ref.at[pl.ds(0, rows)]
        pltpu.make_async_copy(whole, whole, sem).wait()

    def up_copy(phase):
        return pltpu.make_async_remote_copy(
            tops,
            got_bottoms.at[phase],
            up_sem.at[phase, 0],
            up_sem.at[phase, 1],
            device_id={"gz": layer + 1},
            device_id_type=MESH,
        )

    def down_copy(phase):
        return pltpu.make_async_remote_copy(
            bottoms,
            got_tops.at[phase],
            down_sem.at[phase, 0],
            down_sem.at[phase, 1],
            device_id={"gz": layer - 1},
            device_id_type=MESH,
        )

    def start_ends(phase):
        @pl.when(layer < layers - 1)
        def _():
            up_copy(phase).start()

        @pl.when(layer > 0)
        def _():
            down_copy(phase).start()

    def finish_ends(phase):
        @pl.when(layer < layers - 1)
        def _():
            up_copy(phase).wait_send()
            down_copy(phase).wait_recv()

        @pl.when(layer > 0)
        def _():
            down_copy(phase).wait_send()
            up_copy(phase).wait_recv()

    def send_rows(phase, rows):
        for peer in peers:
            pltpu.make_async_remote_copy(
                sent.at[phase, pl.ds(pl.multiple_of(peer * 8, 8), rows)],
                received.at[phase, pl.ds(pl.multiple_of(me * 8, 8), rows)],
                swap_sem.at[phase, 0],
                swap_sem.at[phase, 1],
                device_id=(layer, peer),
                device_id_type=MESH,
            ).start()

    def wait_sent(phase, rows):
        wait_rows(sent.at[phase], others * rows, swap_sem.at[phase, 0])

    def wait_received(phase, rows):
        wait_rows(received.at[phase], others * rows, swap_sem.at[phase, 1])

    def put(phase, first_row, value):
        for pair in range(PAIRS):
            sent[phase, pl.ds(first_row + pair, blocks, stride=8), :] = value[:, lanes_of(pair)]

    def got(phase, row):
        return received[phase, pl.ds(row, blocks, stride=8), :]

    def arrivals(chunk, pair, value):
        for offset, part in enumerate(swap_pair(value[0:64], value[64:128])):
            yield 2 * pair + offset, turned(part, index_to[chunk])

    def end_arrivals(phase):
        for pair in range(PAIRS):
            ends = got_bottoms[phase, rows_of(pair), :], got_tops[phase, rows_of(pair), :]
            for right, part in arrivals(2, pair, jnp.concatenate(ends, axis=0)):
                spot = rows_of(right), lanes_of(2)
                yield spot, jnp.where(live, image[spot] + part, 0.0)

    def keep(ref, spot, value):
        rows, lanes = spot
        ref[spot] = value
        high, low_part = halves(value)
        vector[rows, 2 * lanes.start : 2 * lanes.start + LANES] = high
        vector[rows, 2 * lanes.start + LANES : 2 * lanes.stop] = low_part

    def summed(quantities):
        lanes = lane_of((RIGHT, LANES))
        place = row_of((RIGHT, LANES))
        spread = jnp.zeros((RIGHT, LANES), F32)
        for number, rows in enumerate(quantities):
            total = jnp.sum(jnp.concatenate(rows, axis=0), axis=1, keepdims=True)
            spread = jnp.where(lanes == place + number * RIGHT, total, spread)
        return jnp.sum(spread, axis=0, keepdims=True)

    def share(mine, out_ref, in_ref, place, sem, targets):
        out_ref[...] = mine
        in_ref[place] = mine
        for at, peer in targets:
            pltpu.make_async_remote_copy(
                out_ref,
                in_ref.at[place],
                sem.at[0],
                sem.at[1],
                device_id=(at, peer),
                device_id_type=MESH,
            ).start()

    def shared(in_ref, sem, count):
        wait_rows(in_ref, count, sem.at[1])
        wait_rows(in_ref, count, sem.at[0])
        return jnp.sum(in_ref[...], axis=0)

    def share_near(phase, quantities):
        share(
            summed(quantities),
            near_out.at[phase],
            near_in.at[phase],
            layer * 2 + core,
            near_sem.at[phase],
            column_peers,
        )

    def share_far(phase):
        share(
            shared(near_in.at[phase], near_sem.at[phase], len(column_peers)),
            far_out.at[phase],
            far_in.at[phase],
            me // 2,
            far_sem.at[phase],
            [(layer, peer) for peer in far_peers],
        )

    def columns_of(row, count):
        total = jnp.broadcast_to(row, (RIGHT, LANES))
        lanes = lane_of((RIGHT, LANES))
        place = row_of((RIGHT, LANES))
        return [
            jnp.broadcast_to(
                jnp.sum(
                    jnp.where(lanes == place + number * RIGHT, total, 0.0), axis=1, keepdims=True
                ),
                (RIGHT, LANES),
            )
            for number in range(count)
        ]

    def finish_far(phase, count):
        return columns_of(shared(far_in.at[phase], far_sem.at[phase], len(far_peers)), count)

    def owned_square(values):
        kept = values[0] * values[0] + jnp.where(low, 0.0, values[2] * values[2])
        return jnp.sum(kept, axis=0, keepdims=True)

    def inner_rows(left, right):
        kept = left[0] * right[0] + left[1] * right[1] + left[2] * right[2]
        return jnp.sum(kept, axis=0, keepdims=True)

    def chunks_of(ref, right):
        return [ref[rows_of(right), lanes_of(chunk)] for chunk in range(3)]

    def stacked(chunk):
        return slice(2 * chunk * LANES, 2 * (chunk + 1) * LANES)

    def applied(double_ref, low_ref, chunks):
        return sum(
            dot(vector[:, stacked(chunk)], double_ref[stacked(chunk), :])
            + dot(
                vector[:, 2 * chunk * LANES : (2 * chunk + 1) * LANES], low_ref[lanes_of(chunk), :]
            )
            for chunk in chunks
        )

    def hold(double_ref, low_ref, value):
        high, low_part = halves(value)
        low_ref[...] = low_part
        for chunk in range(3):
            double_ref[stacked(chunk), :] = jnp.concatenate([high[lanes_of(chunk)]] * 2, axis=0)

    def face_values(vector, sides_ref, tops_ref):
        for pair in range(PAIRS):
            for chunk in (0, 2):
                left = turned(vector[rows_of(2 * pair), lanes_of(chunk)], index_from[chunk])
                right = turned(vector[rows_of(2 * pair + 1), lanes_of(chunk)], index_from[chunk])
                even, odd = swap_pair(left, right)
                if chunk == 0:
                    turned_back = jnp.transpose(
                        pick(into_faces, jnp.concatenate([even, odd], axis=0))
                    )
                    target = sides_ref
                else:
                    turned_back = jnp.transpose(odd)
                    target = tops_ref
                for offset in range(2):
                    target[pl.ds(2 * pair + offset, 64, stride=8), :] = turned_back[
                        offset * 64 : (offset + 1) * 64
                    ]

    to_slots(image, (2, 1, 0), stores)
    put(0, 0, pick(to_owner, slots_second[...]))
    pl.semaphore_wait(barrier, others + 2 * (layers - 1))

    send_rows(3, 1)
    send_rows(0, 4)
    start_ends(0)
    solved[...] = dot_three(source_h[...], source_l[...], inverse_h[...], inverse_l[...])
    loads[3].wait()
    hold(operator_hh, operator_l, operator[...])
    for right in range(RIGHT):
        for part in range(4):
            solved[rows_of(right), lanes_of(part)] = solved[rows_of(right), lanes_of(part)] / scales[...]
    hold(merged_thh, merged_tl, jnp.transpose(merged_h[...].astype(F32) + merged_l[...].astype(F32)))
    nearby_first = pick(near, slots_second[...])
    wait_received(3, 1)
    to_holder_f = onehot(got(3, 0).astype(jnp.int32) == first_row[:blocks] + 1)
    to_holder = twice(to_holder_f.astype(BF16))
    from_holder = twice(jnp.transpose(to_holder_f).astype(BF16))

    put(1, 0, pick(to_holder, slots_first[...]))
    send_rows(1, 4)
    wait_received(0, 4)
    for pair in range(PAIRS):
        value = nearby_first[:, lanes_of(pair)] + pick(from_holder, got(0, pair))
        for right, part in arrivals(0, pair, value):
            spot = rows_of(right), lanes_of(0)
            keep(first, spot, image[spot] + part)
    finish_ends(0)
    for spot, value in end_arrivals(0):
        keep(first, spot, value)
    second_image[...] = applied(operator_hh, operator_l, (0, 2))
    nearby_second = pick(near_back, slots_first[...])
    wait_received(1, 4)
    for pair in range(PAIRS):
        value = nearby_second[:, lanes_of(pair)] + pick(from_owner, got(1, pair))
        for right, part in arrivals(1, pair, value):
            spot = rows_of(right), lanes_of(1)
            keep(first, spot, image[spot] + part)

    wait_sent(3, 1)
    wait_sent(0, 4)
    wait_sent(1, 4)

    def finish_image(chunk):
        lanes = lanes_of(chunk)
        more = dot(vector[:, stacked(1)], operator_hh[stacked(1), lanes]) + dot(
            vector[:, 256:384], operator_l[128:256, lanes]
        )
        for right in range(RIGHT):
            spot = rows_of(right), lanes
            image[spot] = (second_image[spot] + more[rows_of(right)]) * scales[...]

    finish_image(1)
    to_slots(image, (1,), stores)
    put(2, 0, pick(to_owner, slots_second[...]))
    send_rows(2, 4)
    finish_image(0)
    finish_image(2)
    squares, curves = [], []
    for right in range(RIGHT):
        mine = chunks_of(first, right)
        squares.append(owned_square(mine))
        curves.append(inner_rows(mine, chunks_of(image, right)))
    share_near(0, [squares, curves])
    to_slots(image, (0, 2), stores)
    put(4, 0, pick(to_holder, slots_first[...]))
    send_rows(4, 4)
    start_ends(1)

    nearby_first = pick(near, slots_second[...])
    nearby_second = pick(near_back, slots_first[...])
    moved_zero[...] = applied(merged_thh, merged_tl, (0, 1, 2))
    face_values(first, sides_zero, tops_zero)
    share_far(0)
    finish_ends(1)
    for spot, value in end_arrivals(1):
        keep(update, spot, value)
    wait_received(2, 4)
    for pair in range(PAIRS):
        value = nearby_first[:, lanes_of(pair)] + pick(from_holder, got(2, pair))
        for right, part in arrivals(0, pair, value):
            spot = rows_of(right), lanes_of(0)
            keep(update, spot, image[spot] + part)
    second_image[...] = applied(operator_hh, operator_l, (0, 2))
    wait_received(4, 4)
    for pair in range(PAIRS):
        value = nearby_second[:, lanes_of(pair)] + pick(from_owner, got(4, pair))
        for right, part in arrivals(1, pair, value):
            spot = rows_of(right), lanes_of(1)
            keep(update, spot, image[spot] + part)
    second_image[...] = second_image[...] + applied(operator_hh, operator_l, (1,))
    wait_sent(2, 4)
    wait_sent(4, 4)

    norm, curve = finish_far(0, 2)
    alpha = norm / curve
    squares, curves = [], []
    for right in range(RIGHT):
        step = alpha[right : right + 1, :]
        before, change = chunks_of(first, right), chunks_of(update, right)
        old, turned_change = chunks_of(image, right), chunks_of(second_image, right)
        mine = [before[chunk] - step * change[chunk] for chunk in range(3)]
        new = [old[chunk] - step * (turned_change[chunk] * scales[...]) for chunk in range(3)]
        squares.append(owned_square(mine))
        curves.append(inner_rows(mine, new))
    share(summed([squares, curves]), pair_out, pair_in, core, pair_sem, [(layer, me - core + 1 - core)])

    share(
        shared(pair_in, pair_sem, 1),
        all_out,
        all_in,
        layer * (blocks // 2) + me // 2,
        all_sem,
        [(at, peer) for _, _, _, c, at, peer in everyone if c == 0],
    )
    moved_one[...] = applied(merged_thh, merged_tl, (0, 1, 2))
    face_values(update, sides_one, tops_one)
    norm_next, curve_next = columns_of(shared(all_in, all_sem, layers * blocks // 2 - 1), 2)
    beta = norm_next / norm
    curve_next = curve_next - beta * norm_next / alpha
    weight_update = norm_next / curve_next
    weights[0:8, :] = alpha + weight_update * beta + weight_update
    weights[8:16, :] = weight_update * alpha


def combine(
    weights,
    solved,
    moved_zero,
    moved_one,
    sides_zero,
    sides_one,
    tops_zero,
    tops_one,
    interior_hbm,
    sides_hbm,
    tops_hbm,
    interior,
    sides,
    tops,
    sem,
):
    writes = []

    def write(here, there, rows):
        writes.append(pltpu.make_async_copy(here.at[rows], there.at[rows], sem.at[len(writes)]))
        writes[-1].start()

    for right in range(RIGHT):
        rows = slice(right * 64, right * 64 + 64)
        for part in range(4):
            spot = rows, slice(part * LANES, part * LANES + LANES)
            interior[spot] = (
                solved[spot]
                - weights[right : right + 1, :] * moved_zero[spot]
                + weights[8 + right : 9 + right, :] * moved_one[spot]
            )
        if right % 2 == 1:
            write(interior, interior_hbm, pl.ds(right * 64 - 64, 128))
    for node in range(64):
        spot = slice(node * 8, node * 8 + 8)
        sides[spot, :] = weights[0:8, :] * sides_zero[spot, :] - weights[8:16, :] * sides_one[spot, :]
        tops[spot, :] = weights[0:8, :64] * tops_zero[spot, :] - weights[8:16, :64] * tops_one[spot, :]
    write(sides, sides_hbm, pl.ds(0, 512))
    write(tops, tops_hbm, pl.ds(0, 512))
    for started in writes:
        started.wait()


def solution(mesh):
    layers, blocks = mesh.shape["gz"], mesh.shape["dev"]

    def per_device(source, inverse, coupling, operator, face_ids, orientation, scale):
        flat = source.transpose(1, 2, 0).reshape(ROWS, NODES)
        vmem = pltpu.VMEM
        far = pl.BlockSpec(memory_space=pltpu.HBM)
        local = pl.BlockSpec(memory_space=pltpu.VMEM)
        dma = pltpu.SemaphoreType.DMA
        shapes = [
            *[jax.ShapeDtypeStruct((ROWS, NODES), F32)] * 3,
            *[jax.ShapeDtypeStruct((512, 128), F32)] * 2,
            *[jax.ShapeDtypeStruct((512, 64), F32)] * 2,
            jax.ShapeDtypeStruct((16, LANES), F32),
        ]
        *found, weights = pl.pallas_call(
            functools.partial(kernel, layers, blocks),
            out_shape=tuple(shapes),
            in_specs=[far] * 7,
            out_specs=(local,) * 8,
            scratch_shapes=[
                vmem((ROWS, NODES), F32),
                vmem((NODES, NODES), F32),
                vmem((NODES, LOCAL), F32),
                vmem((LOCAL, LOCAL), F32),
                vmem((4, ELEMENTS), jnp.int32),
                vmem((6, ELEMENTS), jnp.int32),
                vmem((1, ELEMENTS), jnp.int32),
                *[vmem((ROWS, NODES), BF16)] * 2,
                *[vmem((NODES, NODES), BF16)] * 2,
                *[vmem((NODES, LOCAL), BF16)] * 2,
                vmem((2 * LOCAL, LOCAL), BF16),
                vmem((LOCAL, LOCAL), BF16),
                *[vmem((NODES, LOCAL), BF16)] * 2,
                vmem((2 * LOCAL, NODES), BF16),
                vmem((LOCAL, NODES), BF16),
                vmem((LANES, LANES), F32),
                vmem((3, ELEMENTS, LANES), jnp.int32),
                vmem((3, ELEMENTS, LANES), jnp.int32),
                vmem((ELEMENTS, LANES), F32),
                *[vmem((ROWS, LOCAL), F32)] * 3,
                vmem((ROWS, 2 * LOCAL), BF16),
                *[vmem((128, 512), F32)] * 2,
                *[vmem((256, 128), F32)] * 2,
                vmem((ROWS, LOCAL), F32),
                *[vmem((5, blocks * 8, LANES), F32)] * 2,
                *[vmem((2, 256, 128), F32)] * 2,
                vmem((2, 1, LANES), F32),
                vmem((2, 2 * layers, 1, LANES), F32),
                vmem((2, 1, LANES), F32),
                vmem((2, blocks // 2, 1, LANES), F32),
                vmem((1, LANES), F32),
                vmem((2, 1, LANES), F32),
                vmem((1, LANES), F32),
                vmem((layers * blocks // 2, 1, LANES), F32),
                dma((7,)),
                dma((5, 2)),
                dma((2, 2)),
                dma((2, 2)),
                dma((2, 2)),
                dma((2, 2)),
                dma((2,)),
                dma((2,)),
            ],
            compiler_params=pltpu.CompilerParams(
                collective_id=0, has_side_effects=True, vmem_limit_bytes=32 << 20
            ),
        )(
            *(
                pltpu.with_memory_space_constraint(value, pltpu.HBM)
                for value in (
                    flat,
                    inverse,
                    coupling,
                    operator,
                    face_ids.T,
                    orientation.T,
                    scale.reshape(1, ELEMENTS),
                )
            )
        )
        interior, sides, tops = pl.pallas_call(
            combine,
            out_shape=(shapes[0], shapes[3], shapes[5]),
            in_specs=[local] * 8,
            out_specs=(pl.BlockSpec(memory_space=pl.ANY),) * 3,
            scratch_shapes=[
                vmem((ROWS, NODES), F32),
                vmem((512, 128), F32),
                vmem((512, 64), F32),
                dma((6,)),
            ],
            compiler_params=pltpu.CompilerParams(vmem_limit_bytes=16 << 20),
        )(weights, *found)
        return (
            interior.reshape(RIGHT, ELEMENTS, NODES).transpose(2, 0, 1),
            sides.reshape(64, RIGHT, 128),
            tops.reshape(64, RIGHT, ELEMENTS),
        )

    columns = P(None, None, ("gz", "dev"))
    return jax.shard_map(
        per_device,
        mesh=mesh,
        in_specs=(
            columns,
            P(),
            P(),
            P(),
            P(("gz", "dev"), None),
            P(("gz", "dev"), None),
            P(("gz", "dev")),
        ),
        out_specs=(columns, columns, columns),
        check_vma=False,
    )
```

```python
import functools

import jax
import jax.numpy as jnp
from jax import lax
from jax.experimental import pallas as pl
from jax.experimental.pallas import tpu as pltpu
from jax.sharding import PartitionSpec as P

MESH = pl.DeviceIdType.MESH
F32 = jnp.float32
BF16 = jnp.bfloat16
LANES = 128
ELEMENTS = 64
RIGHT = 8
NODES = 512
LOCAL = 384
ROWS = RIGHT * ELEMENTS
PAIRS = RIGHT // 2


def turns(layers, blocks):
    def ring(step, count):
        return min(step, count - step)

    deep = blocks // 8
    steps = [
        (x, z, y, core)
        for x in range(layers)
        for z in range(deep)
        for y in range(4)
        for core in (1, 0)
        if (x, z, y, core) != (0, 0, 0, 0)
    ]
    return sorted(
        steps, key=lambda step: (-ring(step[0], layers) - ring(step[1], deep) - ring(step[2], 4), step[3])
    )


def halves(value):
    high = value.astype(BF16)
    return high, (value - high.astype(F32)).astype(BF16)


def dot(left, right):
    return jnp.dot(left, right, preferred_element_type=F32)


def dot_three(left_high, left_low, right_high, right_low):
    return dot(left_high, right_high) + (dot(left_high, right_low) + dot(left_low, right_high))


def twice(onehot):
    return jnp.concatenate([onehot, onehot], axis=1)


def pick(onehots, value):
    return dot(onehots, jnp.concatenate(halves(value), axis=0))


def lane_of(shape):
    return lax.broadcasted_iota(jnp.int32, shape, 1)


def row_of(shape):
    return lax.broadcasted_iota(jnp.int32, shape, 0)


def swap_pair(first, second):
    low = lane_of(first.shape) < 64
    return (
        jnp.where(low, first, pltpu.roll(second, 64, 1)),
        jnp.where(low, pltpu.roll(first, 64, 1), second),
    )


def turned(value, index):
    return jnp.take_along_axis(value, index, axis=1, mode="promise_in_bounds")


def kernel(
    layers,
    blocks,
    source_hbm,
    inverse_hbm,
    coupling_hbm,
    operator_hbm,
    faces_hbm,
    codes_hbm,
    scale_hbm,
    solved,
    moved_zero,
    moved_one,
    sides_zero,
    sides_one,
    tops_zero,
    tops_one,
    weights,
    source,
    inverse,
    coupling,
    operator,
    faces_ref,
    codes_ref,
    scale_ref,
    source_h,
    source_l,
    inverse_h,
    inverse_l,
    coupling_h,
    coupling_l,
    operator_hh,
    operator_l,
    merged_h,
    merged_l,
    merged_thh,
    merged_tl,
    table,
    index_to,
    index_from,
    scales,
    first,
    image,
    update,
    vector,
    slots_first,
    slots_second,
    bottoms,
    tops,
    second_image,
    sent,
    received,
    got_bottoms,
    got_tops,
    near_out,
    near_in,
    far_out,
    far_in,
    pair_out,
    pair_in,
    all_out,
    all_in,
    load_sem,
    swap_sem,
    up_sem,
    down_sem,
    near_sem,
    far_sem,
    pair_sem,
    all_sem,
):
    layer = lax.axis_index("gz")
    me = lax.axis_index("dev")
    others = blocks - 1
    core = me % 2

    deep = blocks // 8
    along_x = [(layer + step) % layers for step in range(layers)]
    along_z = [(me // 8 + step) % deep * 8 for step in range(deep)]
    along_y = [(me % 8 // 2 + step) % 4 * 2 for step in range(4)]
    along_core = [core, 1 - core]
    everyone = [
        (x, z, y, c, along_x[x], along_z[z] + along_y[y] + along_core[c])
        for x, z, y, c in turns(layers, blocks)
    ]
    peers = [peer for x, *_, peer in everyone if x == 0]
    column_peers = [(at, peer) for x, z, y, _, at, peer in everyone if z == 0 and y == 0]
    far_peers = [peer for x, _, _, c, _, peer in everyone if x == 0 and c == 0]

    barrier = pltpu.get_barrier_semaphore()
    for peer in peers:
        pl.semaphore_signal(barrier, inc=1, device_id=(layer, peer), device_id_type=MESH)
    for at, peer in column_peers:
        if at is not along_x[0]:
            pl.semaphore_signal(barrier, inc=1, device_id=(at, peer), device_id_type=MESH)

    loads = [
        pltpu.make_async_copy(inverse_hbm, inverse, load_sem.at[0]),
        pltpu.make_async_copy(coupling_hbm, coupling, load_sem.at[1]),
        pltpu.make_async_copy(source_hbm, source, load_sem.at[2]),
        pltpu.make_async_copy(operator_hbm, operator, load_sem.at[3]),
        pltpu.make_async_copy(faces_hbm, faces_ref, load_sem.at[4]),
        pltpu.make_async_copy(codes_hbm, codes_ref, load_sem.at[5]),
        pltpu.make_async_copy(scale_hbm, scale_ref, load_sem.at[6]),
    ]
    for load in loads[4:] + loads[:4]:
        load.start()

    here = pl.ds(pl.multiple_of(me * 8, 8), 8)
    for phase in range(5):
        received[phase, here, :] = jnp.zeros((8, LANES), F32)

    @pl.when(layer == 0)
    def _():
        got_bottoms[...] = jnp.zeros(got_bottoms.shape, F32)

    @pl.when(layer == layers - 1)
    def _():
        got_tops[...] = jnp.zeros(got_tops.shape, F32)

    table[...] = jnp.zeros(table.shape, F32)
    for load in loads[4:]:
        load.wait()
    faces = faces_ref[...].astype(F32)
    codes = codes_ref[...].astype(F32)
    for row in range(2):
        table[row : row + 1, 0:64] = faces[2 * row : 2 * row + 1]
        table[row : row + 1, 64:128] = faces[2 * row + 1 : 2 * row + 2]
    for row in range(3):
        table[2 + row : 3 + row, 0:64] = codes[2 * row : 2 * row + 1]
        table[2 + row : 3 + row, 64:128] = codes[2 * row + 1 : 2 * row + 2]
    table[5:6, 0:64] = scale_ref[...].astype(F32)
    columns = jnp.transpose(table[...])
    square = (LANES, LANES)
    first_row = jnp.broadcast_to(table[0:1, :], square).astype(jnp.int32) - me * LANES
    second_row = jnp.broadcast_to(table[1:2, :], square).astype(jnp.int32)
    first_col = jnp.broadcast_to(columns[:, 0:1], square).astype(jnp.int32) - me * LANES
    second_col = jnp.broadcast_to(columns[:, 1:2], square).astype(jnp.int32)

    def onehot(condition):
        return jnp.where(condition, 1.0, 0.0).astype(F32)

    near = twice(onehot(first_col + me * LANES == second_row).astype(BF16))
    near_back = twice(onehot(first_row + me * LANES == second_col).astype(BF16))
    into_faces = twice(onehot(first_row == row_of(square)).astype(BF16))
    peer_shape = (blocks, LANES)
    owner_row = second_row[:blocks] // LANES
    peer_row = row_of(peer_shape)
    to_owner_f = onehot((owner_row == peer_row) & (peer_row != me))
    to_owner = twice(to_owner_f.astype(BF16))
    from_owner = twice(jnp.transpose(to_owner_f).astype(BF16))
    slot_number = (second_row[:blocks] % LANES + 1).astype(F32)
    named = jnp.sum(to_owner_f * slot_number, axis=1, keepdims=True)
    sent[3, pl.ds(0, blocks, stride=8), :] = jnp.broadcast_to(named, peer_shape)

    lane = lane_of((ELEMENTS, LANES))
    low = lane < 64
    node_a, node_b = lane % 64 // 8, lane % 8
    for chunk in range(3):
        code = jnp.where(
            low,
            jnp.broadcast_to(columns[0:64, 2 + chunk : 3 + chunk], lane.shape),
            jnp.broadcast_to(columns[64:128, 2 + chunk : 3 + chunk], lane.shape),
        ).astype(jnp.int32)
        swapped, flip_a, flip_b = code // 4 % 2 == 1, code // 2 % 2 == 1, code % 2 == 1
        half = lane // 64 * 64
        a = jnp.where(flip_a, 7 - node_a, node_a)
        b = jnp.where(flip_b, 7 - node_b, node_b)
        index_to[chunk] = half + jnp.where(swapped, b * 8 + a, a * 8 + b)
        a = jnp.where(swapped, node_b, node_a)
        b = jnp.where(swapped, node_a, node_b)
        index_from[chunk] = half + jnp.where(flip_a, 7 - a, a) * 8 + jnp.where(flip_b, 7 - b, b)
    scales[...] = jnp.broadcast_to(columns[0:64, 5:6], scales.shape)
    live = (low & (layer > 0)) | ((lane >= 64) & (layer < layers - 1))

    def rows_of(right):
        return slice(right * ELEMENTS, (right + 1) * ELEMENTS)

    def lanes_of(chunk):
        return slice(chunk * LANES, (chunk + 1) * LANES)

    loads[0].wait()
    inverse_h[...], inverse_l[...] = halves(inverse[...])
    loads[1].wait()
    coupling_h[...], coupling_l[...] = halves(coupling[...])
    merged = dot_three(inverse_h[...], inverse_l[...], coupling_h[...], coupling_l[...])
    merged_h[...], merged_l[...] = halves(merged)
    loads[2].wait()
    source_h[...], source_l[...] = halves(source[...])
    image[...] = dot_three(source_h[...], source_l[...], merged_h[...], merged_l[...])

    def to_slots(vector, chunks, stores):
        for chunk in chunks:
            for pair in range(PAIRS):
                left = turned(vector[rows_of(2 * pair), lanes_of(chunk)], index_from[chunk])
                right = turned(vector[rows_of(2 * pair + 1), lanes_of(chunk)], index_from[chunk])
                stores[chunk](pair, *swap_pair(left, right))

    def store_slots(ref):
        def store(pair, even, odd):
            ref[0:64, lanes_of(pair)] = even
            ref[64:128, lanes_of(pair)] = odd

        return store

    def store_ends(pair, even, odd):
        bottoms[rows_of(pair), :] = even
        tops[rows_of(pair), :] = odd

    stores = (store_slots(slots_first), store_slots(slots_second), store_ends)

    def wait_rows(ref, rows, sem):
        whole = ref.at[pl.ds(0, rows)]
        pltpu.make_async_copy(whole, whole, sem).wait()

    def up_copy(phase):
        return pltpu.make_async_remote_copy(
            tops,
            got_bottoms.at[phase],
            up_sem.at[phase, 0],
            up_sem.at[phase, 1],
            device_id={"gz": layer + 1},
            device_id_type=MESH,
        )

    def down_copy(phase):
        return pltpu.make_async_remote_copy(
            bottoms,
            got_tops.at[phase],
            down_sem.at[phase, 0],
            down_sem.at[phase, 1],
            device_id={"gz": layer - 1},
            device_id_type=MESH,
        )

    def start_ends(phase):
        @pl.when(layer < layers - 1)
        def _():
            up_copy(phase).start()

        @pl.when(layer > 0)
        def _():
            down_copy(phase).start()

    def finish_ends(phase):
        @pl.when(layer < layers - 1)
        def _():
            up_copy(phase).wait_send()
            down_copy(phase).wait_recv()

        @pl.when(layer > 0)
        def _():
            down_copy(phase).wait_send()
            up_copy(phase).wait_recv()

    def send_rows(phase, rows):
        for peer in peers:
            pltpu.make_async_remote_copy(
                sent.at[phase, pl.ds(pl.multiple_of(peer * 8, 8), rows)],
                received.at[phase, pl.ds(pl.multiple_of(me * 8, 8), rows)],
                swap_sem.at[phase, 0],
                swap_sem.at[phase, 1],
                device_id=(layer, peer),
                device_id_type=MESH,
            ).start()

    def wait_sent(phase, rows):
        wait_rows(sent.at[phase], others * rows, swap_sem.at[phase, 0])

    def wait_received(phase, rows):
        wait_rows(received.at[phase], others * rows, swap_sem.at[phase, 1])

    def put(phase, first_row, value):
        for pair in range(PAIRS):
            sent[phase, pl.ds(first_row + pair, blocks, stride=8), :] = value[:, lanes_of(pair)]

    def got(phase, row):
        return received[phase, pl.ds(row, blocks, stride=8), :]

    def arrivals(chunk, pair, value):
        for offset, part in enumerate(swap_pair(value[0:64], value[64:128])):
            yield 2 * pair + offset, turned(part, index_to[chunk])

    def end_arrivals(phase):
        for pair in range(PAIRS):
            ends = got_bottoms[phase, rows_of(pair), :], got_tops[phase, rows_of(pair), :]
            for right, part in arrivals(2, pair, jnp.concatenate(ends, axis=0)):
                spot = rows_of(right), lanes_of(2)
                yield spot, jnp.where(live, image[spot] + part, 0.0)

    def keep(ref, spot, value):
        rows, lanes = spot
        ref[spot] = value
        high, low_part = halves(value)
        vector[rows, 2 * lanes.start : 2 * lanes.start + LANES] = high
        vector[rows, 2 * lanes.start + LANES : 2 * lanes.stop] = low_part

    def summed(quantities):
        lanes = lane_of((RIGHT, LANES))
        place = row_of((RIGHT, LANES))
        spread = jnp.zeros((RIGHT, LANES), F32)
        for number, rows in enumerate(quantities):
            total = jnp.sum(jnp.concatenate(rows, axis=0), axis=1, keepdims=True)
            spread = jnp.where(lanes == place + number * RIGHT, total, spread)
        return jnp.sum(spread, axis=0, keepdims=True)

    def share(mine, out_ref, in_ref, place, sem, targets):
        out_ref[...] = mine
        in_ref[place] = mine
        for at, peer in targets:
            pltpu.make_async_remote_copy(
                out_ref,
                in_ref.at[place],
                sem.at[0],
                sem.at[1],
                device_id=(at, peer),
                device_id_type=MESH,
            ).start()

    def shared(in_ref, sem, count):
        wait_rows(in_ref, count, sem.at[1])
        wait_rows(in_ref, count, sem.at[0])
        return jnp.sum(in_ref[...], axis=0)

    def share_near(phase, quantities):
        share(
            summed(quantities),
            near_out.at[phase],
            near_in.at[phase],
            layer * 2 + core,
            near_sem.at[phase],
            column_peers,
        )

    def share_far(phase):
        share(
            shared(near_in.at[phase], near_sem.at[phase], len(column_peers)),
            far_out.at[phase],
            far_in.at[phase],
            me // 2,
            far_sem.at[phase],
            [(layer, peer) for peer in far_peers],
        )

    def columns_of(row, count):
        total = jnp.broadcast_to(row, (RIGHT, LANES))
        lanes = lane_of((RIGHT, LANES))
        place = row_of((RIGHT, LANES))
        return [
            jnp.broadcast_to(
                jnp.sum(
                    jnp.where(lanes == place + number * RIGHT, total, 0.0), axis=1, keepdims=True
                ),
                (RIGHT, LANES),
            )
            for number in range(count)
        ]

    def finish_far(phase, count):
        return columns_of(shared(far_in.at[phase], far_sem.at[phase], len(far_peers)), count)

    def owned_square(values):
        kept = values[0] * values[0] + jnp.where(low, 0.0, values[2] * values[2])
        return jnp.sum(kept, axis=0, keepdims=True)

    def inner_rows(left, right):
        kept = left[0] * right[0] + left[1] * right[1] + left[2] * right[2]
        return jnp.sum(kept, axis=0, keepdims=True)

    def chunks_of(ref, right):
        return [ref[rows_of(right), lanes_of(chunk)] for chunk in range(3)]

    def stacked(chunk):
        return slice(2 * chunk * LANES, 2 * (chunk + 1) * LANES)

    def applied(double_ref, low_ref, chunks):
        return sum(
            dot(vector[:, stacked(chunk)], double_ref[stacked(chunk), :])
            + dot(
                vector[:, 2 * chunk * LANES : (2 * chunk + 1) * LANES], low_ref[lanes_of(chunk), :]
            )
            for chunk in chunks
        )

    def hold(double_ref, low_ref, value):
        high, low_part = halves(value)
        low_ref[...] = low_part
        for chunk in range(3):
            double_ref[stacked(chunk), :] = jnp.concatenate([high[lanes_of(chunk)]] * 2, axis=0)

    def face_values(vector, sides_ref, tops_ref):
        for pair in range(PAIRS):
            for chunk in (0, 2):
                left = turned(vector[rows_of(2 * pair), lanes_of(chunk)], index_from[chunk])
                right = turned(vector[rows_of(2 * pair + 1), lanes_of(chunk)], index_from[chunk])
                even, odd = swap_pair(left, right)
                if chunk == 0:
                    turned_back = jnp.transpose(
                        pick(into_faces, jnp.concatenate([even, odd], axis=0))
                    )
                    target = sides_ref
                else:
                    turned_back = jnp.transpose(odd)
                    target = tops_ref
                for offset in range(2):
                    target[pl.ds(2 * pair + offset, 64, stride=8), :] = turned_back[
                        offset * 64 : (offset + 1) * 64
                    ]

    pl.semaphore_wait(barrier, others + 2 * (layers - 1))

    send_rows(3, 1)
    to_slots(image, (1, 0, 2), stores)
    put(0, 0, pick(to_owner, slots_second[...]))
    send_rows(0, 4)
    start_ends(0)
    solved[...] = dot_three(source_h[...], source_l[...], inverse_h[...], inverse_l[...])
    loads[3].wait()
    hold(operator_hh, operator_l, operator[...])
    for right in range(RIGHT):
        for part in range(4):
            solved[rows_of(right), lanes_of(part)] = solved[rows_of(right), lanes_of(part)] / scales[...]
    hold(merged_thh, merged_tl, jnp.transpose(merged_h[...].astype(F32) + merged_l[...].astype(F32)))
    nearby_first = pick(near, slots_second[...])
    wait_received(3, 1)
    to_holder_f = onehot(got(3, 0).astype(jnp.int32) == first_row[:blocks] + 1)
    to_holder = twice(to_holder_f.astype(BF16))
    from_holder = twice(jnp.transpose(to_holder_f).astype(BF16))

    put(1, 0, pick(to_holder, slots_first[...]))
    send_rows(1, 4)
    wait_received(0, 4)
    for pair in range(PAIRS):
        value = nearby_first[:, lanes_of(pair)] + pick(from_holder, got(0, pair))
        for right, part in arrivals(0, pair, value):
            spot = rows_of(right), lanes_of(0)
            keep(first, spot, image[spot] + part)
    finish_ends(0)
    for spot, value in end_arrivals(0):
        keep(first, spot, value)
    second_image[...] = applied(operator_hh, operator_l, (0, 2))
    nearby_second = pick(near_back, slots_first[...])
    wait_received(1, 4)
    for pair in range(PAIRS):
        value = nearby_second[:, lanes_of(pair)] + pick(from_owner, got(1, pair))
        for right, part in arrivals(1, pair, value):
            spot = rows_of(right), lanes_of(1)
            keep(first, spot, image[spot] + part)

    wait_sent(3, 1)
    wait_sent(0, 4)
    wait_sent(1, 4)

    def finish_image(chunk):
        lanes = lanes_of(chunk)
        more = dot(vector[:, stacked(1)], operator_hh[stacked(1), lanes]) + dot(
            vector[:, 256:384], operator_l[128:256, lanes]
        )
        for right in range(RIGHT):
            spot = rows_of(right), lanes
            image[spot] = (second_image[spot] + more[rows_of(right)]) * scales[...]

    finish_image(1)
    to_slots(image, (1,), stores)
    put(2, 0, pick(to_owner, slots_second[...]))
    send_rows(2, 4)
    finish_image(0)
    finish_image(2)
    squares, curves = [], []
    for right in range(RIGHT):
        mine = chunks_of(first, right)
        squares.append(owned_square(mine))
        curves.append(inner_rows(mine, chunks_of(image, right)))
    share_near(0, [squares, curves])
    to_slots(image, (0, 2), stores)
    put(4, 0, pick(to_holder, slots_first[...]))
    send_rows(4, 4)
    start_ends(1)

    nearby_first = pick(near, slots_second[...])
    nearby_second = pick(near_back, slots_first[...])
    moved_zero[...] = applied(merged_thh, merged_tl, (0, 1, 2))
    face_values(first, sides_zero, tops_zero)
    share_far(0)
    finish_ends(1)
    for spot, value in end_arrivals(1):
        keep(update, spot, value)
    wait_received(2, 4)
    for pair in range(PAIRS):
        value = nearby_first[:, lanes_of(pair)] + pick(from_holder, got(2, pair))
        for right, part in arrivals(0, pair, value):
            spot = rows_of(right), lanes_of(0)
            keep(update, spot, image[spot] + part)
    second_image[...] = applied(operator_hh, operator_l, (0, 2))
    wait_received(4, 4)
    for pair in range(PAIRS):
        value = nearby_second[:, lanes_of(pair)] + pick(from_owner, got(4, pair))
        for right, part in arrivals(1, pair, value):
            spot = rows_of(right), lanes_of(1)
            keep(update, spot, image[spot] + part)
    second_image[...] = second_image[...] + applied(operator_hh, operator_l, (1,))
    wait_sent(2, 4)
    wait_sent(4, 4)

    norm, curve = finish_far(0, 2)
    alpha = norm / curve
    squares, curves = [], []
    for right in range(RIGHT):
        step = alpha[right : right + 1, :]
        before, change = chunks_of(first, right), chunks_of(update, right)
        old, turned_change = chunks_of(image, right), chunks_of(second_image, right)
        mine = [before[chunk] - step * change[chunk] for chunk in range(3)]
        new = [old[chunk] - step * (turned_change[chunk] * scales[...]) for chunk in range(3)]
        squares.append(owned_square(mine))
        curves.append(inner_rows(mine, new))
    share(summed([squares, curves]), pair_out, pair_in, core, pair_sem, [(layer, me - core + 1 - core)])

    share(
        shared(pair_in, pair_sem, 1),
        all_out,
        all_in,
        layer * (blocks // 2) + me // 2,
        all_sem,
        [(at, peer) for _, _, _, c, at, peer in everyone if c == 0],
    )
    moved_one[...] = applied(merged_thh, merged_tl, (0, 1, 2))
    face_values(update, sides_one, tops_one)
    norm_next, curve_next = columns_of(shared(all_in, all_sem, layers * blocks // 2 - 1), 2)
    beta = norm_next / norm
    curve_next = curve_next - beta * norm_next / alpha
    weight_update = norm_next / curve_next
    weights[0:8, :] = alpha + weight_update * beta + weight_update
    weights[8:16, :] = weight_update * alpha


def combine(
    weights,
    solved,
    moved_zero,
    moved_one,
    sides_zero,
    sides_one,
    tops_zero,
    tops_one,
    interior_hbm,
    sides_hbm,
    tops_hbm,
    interior,
    sides,
    tops,
    sem,
):
    writes = []

    def write(here, there, rows):
        writes.append(pltpu.make_async_copy(here.at[rows], there.at[rows], sem.at[len(writes)]))
        writes[-1].start()

    for right in range(RIGHT):
        rows = slice(right * 64, right * 64 + 64)
        for part in range(4):
            spot = rows, slice(part * LANES, part * LANES + LANES)
            interior[spot] = (
                solved[spot]
                - weights[right : right + 1, :] * moved_zero[spot]
                + weights[8 + right : 9 + right, :] * moved_one[spot]
            )
        if right % 2 == 1:
            write(interior, interior_hbm, pl.ds(right * 64 - 64, 128))
    for node in range(64):
        spot = slice(node * 8, node * 8 + 8)
        sides[spot, :] = weights[0:8, :] * sides_zero[spot, :] - weights[8:16, :] * sides_one[spot, :]
        tops[spot, :] = weights[0:8, :64] * tops_zero[spot, :] - weights[8:16, :64] * tops_one[spot, :]
    write(sides, sides_hbm, pl.ds(0, 512))
    write(tops, tops_hbm, pl.ds(0, 512))
    for started in writes:
        started.wait()


def solution(mesh):
    layers, blocks = mesh.shape["gz"], mesh.shape["dev"]

    def per_device(source, inverse, coupling, operator, face_ids, orientation, scale):
        flat = source.transpose(1, 2, 0).reshape(ROWS, NODES)
        vmem = pltpu.VMEM
        far = pl.BlockSpec(memory_space=pltpu.HBM)
        local = pl.BlockSpec(memory_space=pltpu.VMEM)
        dma = pltpu.SemaphoreType.DMA
        shapes = [
            *[jax.ShapeDtypeStruct((ROWS, NODES), F32)] * 3,
            *[jax.ShapeDtypeStruct((512, 128), F32)] * 2,
            *[jax.ShapeDtypeStruct((512, 64), F32)] * 2,
            jax.ShapeDtypeStruct((16, LANES), F32),
        ]
        *found, weights = pl.pallas_call(
            functools.partial(kernel, layers, blocks),
            out_shape=tuple(shapes),
            in_specs=[far] * 7,
            out_specs=(local,) * 8,
            scratch_shapes=[
                vmem((ROWS, NODES), F32),
                vmem((NODES, NODES), F32),
                vmem((NODES, LOCAL), F32),
                vmem((LOCAL, LOCAL), F32),
                vmem((4, ELEMENTS), jnp.int32),
                vmem((6, ELEMENTS), jnp.int32),
                vmem((1, ELEMENTS), jnp.int32),
                *[vmem((ROWS, NODES), BF16)] * 2,
                *[vmem((NODES, NODES), BF16)] * 2,
                *[vmem((NODES, LOCAL), BF16)] * 2,
                vmem((2 * LOCAL, LOCAL), BF16),
                vmem((LOCAL, LOCAL), BF16),
                *[vmem((NODES, LOCAL), BF16)] * 2,
                vmem((2 * LOCAL, NODES), BF16),
                vmem((LOCAL, NODES), BF16),
                vmem((LANES, LANES), F32),
                vmem((3, ELEMENTS, LANES), jnp.int32),
                vmem((3, ELEMENTS, LANES), jnp.int32),
                vmem((ELEMENTS, LANES), F32),
                *[vmem((ROWS, LOCAL), F32)] * 3,
                vmem((ROWS, 2 * LOCAL), BF16),
                *[vmem((128, 512), F32)] * 2,
                *[vmem((256, 128), F32)] * 2,
                vmem((ROWS, LOCAL), F32),
                *[vmem((5, blocks * 8, LANES), F32)] * 2,
                *[vmem((2, 256, 128), F32)] * 2,
                vmem((2, 1, LANES), F32),
                vmem((2, 2 * layers, 1, LANES), F32),
                vmem((2, 1, LANES), F32),
                vmem((2, blocks // 2, 1, LANES), F32),
                vmem((1, LANES), F32),
                vmem((2, 1, LANES), F32),
                vmem((1, LANES), F32),
                vmem((layers * blocks // 2, 1, LANES), F32),
                dma((7,)),
                dma((5, 2)),
                dma((2, 2)),
                dma((2, 2)),
                dma((2, 2)),
                dma((2, 2)),
                dma((2,)),
                dma((2,)),
            ],
            compiler_params=pltpu.CompilerParams(
                collective_id=0, has_side_effects=True, vmem_limit_bytes=32 << 20
            ),
        )(
            *(
                pltpu.with_memory_space_constraint(value, pltpu.HBM)
                for value in (
                    flat,
                    inverse,
                    coupling,
                    operator,
                    face_ids.T,
                    orientation.T,
                    scale.reshape(1, ELEMENTS),
                )
            )
        )
        interior, sides, tops = pl.pallas_call(
            combine,
            out_shape=(shapes[0], shapes[3], shapes[5]),
            in_specs=[local] * 8,
            out_specs=(pl.BlockSpec(memory_space=pl.ANY),) * 3,
            scratch_shapes=[
                vmem((ROWS, NODES), F32),
                vmem((512, 128), F32),
                vmem((512, 64), F32),
                dma((6,)),
            ],
            compiler_params=pltpu.CompilerParams(vmem_limit_bytes=16 << 20),
        )(weights, *found)
        return (
            interior.reshape(RIGHT, ELEMENTS, NODES).transpose(2, 0, 1),
            sides.reshape(64, RIGHT, 128),
            tops.reshape(64, RIGHT, ELEMENTS),
        )

    columns = P(None, None, ("gz", "dev"))
    return jax.shard_map(
        per_device,
        mesh=mesh,
        in_specs=(
            columns,
            P(),
            P(),
            P(),
            P(("gz", "dev"), None),
            P(("gz", "dev"), None),
            P(("gz", "dev")),
        ),
        out_specs=(columns, columns, columns),
        check_vma=False,
    )
```
